256 devices in a mesh: pix: 32 (over z, y), shell: 8 (over x, core).
Axes of the slice: x: 4, y: 4, z: 8, core: 2. Of those that a mesh axis runs over, the one named last changes fastest.
Arguments:
- field: float32 [128, 1048576], P('shell', 'pix'), may hold values from -3 to 3
- momentum: float32 [128, 1048576], P('shell', 'pix'), may hold values from -6 to 6
- kernels: float32 [4, 20, 128], P(None, None, 'shell'), may hold values from 0.002 to 0.02
- depth_class: int32 [1048576], P('pix'), may hold values from 0 to 3
- counts: int32 [20, 1048576], P(None, 'pix'), may hold values from 0 to 12
- mask: float32 [1048576], P('pix'), may hold values from 0.1 to 1.5, as said below
- mean_counts: float32 [20], replicated, may hold values from 1 to 8
- shell_scale: float32 [128], P('shell'), may hold values from 0.5 to 2
Outputs:
- gradient: float32 [128, 1048576], P('shell', 'pix')
- loglik: float32 [], replicated
The draws below stay inside these ranges and needn't reach their ends.
Inputs may be any that keep to these rules, and one draw needn't show every extreme that they name: `mask`: mask weights are positive.
All inputs are finite; a program needn't handle non-finite values.
Results may differ from the reference program's by a relative error of at most 0.00005.
Values sent between devices are 32-bit elements; how exact they have to be, the bound alone decides.
No kernel may reach another device: no remote copies, remote signals or barrier semaphores. Data moves between devices by JAX's collectives and lax.ppermute only.
A program may use at most 128 MiB of HBM per device.

```python
import math
import jax
import jax.numpy as jnp
from jax import lax

SHELLS = 128
BINS = 20
CLASSES = 4
CYCLE = 2048
PIX = 1048576


def draw_mask(key, part):
    position = jnp.arange(PIX, dtype=jnp.float32) / PIX
    base = 0.5 + position
    factor = jax.random.uniform(key, (PIX,), jnp.float32, 0.4, 1.0)
    return base * factor


def with_ends(result, own_key, low, largest):
    place = [jax.random.randint(jax.random.fold_in(own_key, axis), (), 0, length) for axis, length in enumerate(result.shape)]
    main_axis = result.shape.index(max(result.shape))
    neighbour = place[:main_axis] + [(place[main_axis] + 1) % result.shape[main_axis]] + place[main_axis + 1:]
    return result.at[tuple(place)].set(low).at[tuple(neighbour)].set(largest)


def shard_levels(own_key, extent, pieces, smallest, top_value):
    loudness, own = 1.0, jax.random.fold_in(own_key, 6)
    for axis_at, blocks in pieces:
        steps = jnp.exp(jax.random.uniform(jax.random.fold_in(own, axis_at), (blocks,), jnp.float32, smallest / len(pieces), top_value / len(pieces)))
        loudness = loudness * jnp.repeat(steps, extent[axis_at] // blocks).reshape([-1 if axis == axis_at else 1 for axis in range(len(extent))])
    return loudness


def bell_draw(own_key, extent, width, most, pieces=(), held_as=jnp.bfloat16):
    level = shard_levels(own_key, extent, pieces, -0.22, 0.18) if pieces else 1.0
    array = jax.random.normal(own_key, extent, jnp.float32) * width * level
    return jnp.minimum(jnp.maximum(array, -most), most).astype(held_as)


def setup_inputs(seed: int = 0) -> dict:
    arg_keys = jax.random.split(jax.random.key(seed), 9)
    field = bell_draw(arg_keys[0], (SHELLS, PIX), 0.5, 3.0, ((0, 8), (1, 32)), jnp.float32)
    momentum = bell_draw(arg_keys[1], (SHELLS, PIX), 1.0, 6.0, ((0, 8), (1, 32)), jnp.float32)
    kernels = jnp.clip(jnp.exp(math.log(0.02) - 2.30258502 * jax.random.uniform(arg_keys[2], (CLASSES, BINS, SHELLS), jnp.float32) ** shard_levels(arg_keys[2], (CLASSES, BINS, SHELLS), ((2, 8),), -0.2, 0.2)), 0.002, 0.02)
    depth_class = with_ends(jax.random.randint(arg_keys[3], (PIX,), 0, CLASSES), jax.random.fold_in(arg_keys[3], 1), 0, CLASSES - 1).astype(jnp.int32)
    counts = with_ends(jax.random.randint(arg_keys[4], (BINS, PIX), 0, 13), jax.random.fold_in(arg_keys[4], 1), 0, 12).astype(jnp.int32)
    mask = draw_mask(jax.random.fold_in(arg_keys[8], 71), 0)
    mean_counts = jnp.clip(jnp.exp(jax.random.uniform(arg_keys[6], (BINS,), jnp.float32, math.log(1.0), math.log(8.0))), 1.0, 8.0)
    shell_scale = jnp.clip(jnp.exp(math.log(2.0) - 1.3862944 * jax.random.uniform(arg_keys[7], (SHELLS,), jnp.float32) ** shard_levels(arg_keys[7], (SHELLS,), ((0, 8),), -0.2, 0.2)), 0.5, 2.0)
    return {"field": field, "momentum": momentum, "kernels": kernels, "depth_class": depth_class, "counts": counts, "mask": mask, "mean_counts": mean_counts, "shell_scale": shell_scale}


LEAP = 0.1
ANGULAR = 0.5
RADIAL = 0.5


def reference(field, momentum, kernels, depth_class, counts, mask, mean_counts, shell_scale):
    position = field + LEAP * momentum
    density = jnp.exp(position)
    flat = kernels.reshape(CLASSES * BINS, SHELLS)
    onehot = (depth_class[None, :] == jnp.arange(CLASSES, dtype=jnp.int32)[:, None]).astype(jnp.float32)
    every = jnp.dot(flat, density, precision=lax.Precision.HIGHEST, preferred_element_type=jnp.float32)
    proj = jnp.sum(every.reshape(CLASSES, BINS, PIX) * onehot[:, None, :], axis=0)
    weighted = jnp.sum(mask[None, :] * proj, axis=1)
    norm = weighted / PIX
    counted = counts.astype(jnp.float32)
    total = jnp.sum(counted, axis=1)
    rate = mean_counts[:, None] * mask[None, :] * proj / norm[:, None]
    loglik = jnp.sum(counted * jnp.log(rate) - rate) / (BINS * PIX)
    ratio = counted / proj - (total / (PIX * norm))[:, None] * mask[None, :]
    spread = (onehot[:, None, :] * ratio[None, :, :]).reshape(CLASSES * BINS, PIX)
    back = jnp.dot(flat.T, spread, precision=lax.Precision.HIGHEST, preferred_element_type=jnp.float32)
    like = density * back
    padded = jnp.pad(position, ((0, 0), (CYCLE, CYCLE)))
    angular = 4.0 * position - padded[:, CYCLE - 1:CYCLE - 1 + PIX] - padded[:, CYCLE + 1:CYCLE + 1 + PIX]
    angular = angular - padded[:, 0:PIX] - padded[:, 2 * CYCLE:2 * CYCLE + PIX]
    stacked = jnp.pad(position, ((1, 1), (0, 0)))
    radial = 2.0 * position - stacked[:-2] - stacked[2:]
    gradient = like - position / (shell_scale[:, None] * shell_scale[:, None]) - ANGULAR * angular - RADIAL * radial
    return gradient, loglik
```

```python
import functools

import jax
import jax.numpy as jnp
from jax import lax
from jax.experimental import pallas as pl
from jax.experimental.pallas import tpu as pltpu
from jax.sharding import PartitionSpec as P

CYCLE = 2048
LEAP = 0.1
ANGULAR = 0.5
RADIAL = 0.5
WIDE = 256


def split(values):
    high = values.astype(jnp.bfloat16)
    low = (values - high.astype(jnp.float32)).astype(jnp.bfloat16)
    return high, low


def iota(shape, dim):
    return lax.broadcasted_iota(jnp.int32, shape, dim)


def dot_nt(a, b):
    return lax.dot_general(a, b, (((1,), (1,)), ((), ())), preferred_element_type=jnp.float32)


def forward_weights(table, classes, bins, shells):
    rows, cols = classes * 2 * bins, 6 * shells
    spread = (iota((rows, bins), 0) % bins == iota((rows, bins), 1)).astype(jnp.bfloat16)
    same_class = iota((rows, classes * shells), 0) // (2 * bins) == (
        iota((rows, classes * shells), 1) // shells
    )
    place = (iota((classes * shells, cols), 0) % shells == iota((classes * shells, cols), 1) % shells)
    place = place.astype(jnp.bfloat16)
    parts = []
    for part in split(table):
        wide = jnp.where(same_class, dot_nt(spread, part), 0.0).astype(jnp.bfloat16)
        parts.append(jnp.dot(wide, place, preferred_element_type=jnp.float32))
    row, col = iota((rows, cols), 0), iota((rows, cols), 1)
    picked = jnp.where(col // (2 * shells) == 2, parts[1], parts[0])
    same_sub = (row // bins) % 2 == (col // shells) % 2
    return jnp.where(same_sub, picked, 0.0).astype(jnp.bfloat16)


def backward_weights(table, classes, bins, shells, depth):
    half = classes * shells
    rows, cols = 2 * half, 3 * depth
    place = iota((bins, cols), 0) == (iota((bins, cols), 1) % depth) % bins
    place = place.astype(jnp.bfloat16)
    parts = []
    for part in split(table):
        once = jnp.dot(part, place, preferred_element_type=jnp.float32)
        parts.append(jnp.concatenate([once, once], axis=0))
    row, col = iota((rows, cols), 0), iota((rows, cols), 1)
    picked = jnp.where(col // depth == 2, parts[1], parts[0])
    same_sub = row // half == (col % depth) // bins
    return jnp.where(same_sub, picked, 0.0).astype(jnp.bfloat16)


def packed_row(row, columns, sub_width, bins):
    width = columns.stop - columns.start
    first = row[:, columns]
    second = row[:, columns.start + sub_width : columns.stop + sub_width]
    return jnp.where(iota((2 * bins, width), 0) < bins, first, second)


def project_body(
    pieces, field, momentum, depth, mask, table, proj, density, weighted, weights, classes, bins
):
    shells, width = field.shape
    sub = width // 2

    @pl.when(pl.program_id(0) == 0)
    def _():
        weights[...] = forward_weights(table[...], classes, bins, shells)
        weighted[...] = jnp.zeros_like(weighted)

    total = jnp.zeros(weighted.shape, jnp.float32)
    depth_row, mask_row = depth[...], mask[...]
    for start in range(0, sub, WIDE):
        halves = []
        for base in (start, start + sub):
            here = slice(base, base + WIDE)
            values = jnp.exp(field[:, here] + LEAP * momentum[:, here])
            density[:, here] = values
            halves.append(values)
        high, low = split(jnp.concatenate(halves, axis=0))
        every = jnp.dot(
            weights[...],
            jnp.concatenate([high, low, high], axis=0),
            preferred_element_type=jnp.float32,
        )
        here = slice(start, start + WIDE)
        chosen = packed_row(depth_row, here, sub, bins)
        picked = every[: 2 * bins]
        for k in range(1, classes):
            picked = jnp.where(chosen == k, every[2 * bins * k : 2 * bins * (k + 1)], picked)
        proj[0, :, here] = picked
        scaled = picked * packed_row(mask_row, here, sub, bins)
        for lane in range(0, WIDE, 128):
            total = total + scaled[:, lane : lane + 128]
    weighted[...] += total


def project(pieces, field, momentum, depth, mask, table, classes, bins):
    shells, pixels = field.shape
    count = pieces.shape[0]
    width = pixels // 8
    here = lambda i, where: (0, where[i])
    return pl.pallas_call(
        functools.partial(project_body, classes=classes, bins=bins),
        grid_spec=pltpu.PrefetchScalarGridSpec(
            num_scalar_prefetch=1,
            grid=(count,),
            in_specs=[
                pl.BlockSpec((shells, width), here),
                pl.BlockSpec((shells, width), here),
                pl.BlockSpec((1, width), here),
                pl.BlockSpec((1, width), here),
                pl.BlockSpec(table.shape, lambda i, where: (0, 0)),
            ],
            out_specs=[
                pl.BlockSpec((1, 2 * bins, width // 2), lambda i, where: (i, 0, 0)),
                pl.BlockSpec((shells, width), lambda i, where: (0, i)),
                pl.BlockSpec((2 * bins, 128), lambda i, where: (0, 0)),
            ],
            scratch_shapes=[pltpu.VMEM((classes * 2 * bins, 6 * shells), jnp.bfloat16)],
        ),
        out_shape=[
            jax.ShapeDtypeStruct((count, 2 * bins, width // 2), jnp.float32),
            jax.ShapeDtypeStruct((shells, count * width), jnp.float32),
            jax.ShapeDtypeStruct((2 * bins, 128), jnp.float32),
        ],
        name="project",
    )(pieces, field, momentum, depth, mask, table)


def stencil_body(
    field, momentum, before, after, above, below, scale, counts, out, totals, position
):
    shells, pixels = field.shape
    position[:, :CYCLE] = before[...]
    position[:, CYCLE + pixels :] = after[...]
    for start in range(0, pixels, CYCLE):
        here = slice(start, start + CYCLE)
        position[:, CYCLE + start : 2 * CYCLE + start] = field[:, here] + LEAP * momentum[:, here]
    square = scale[...] * scale[...]
    row = iota((shells, 512), 0)
    totals[...] = jnp.zeros_like(totals)

    def step(i, carry):
        start = pl.multiple_of(i * 512, 512)
        near = position[:, pl.ds(CYCLE + start - 128, 512 + 256)]
        middle = near[:, 128:640]
        left = pltpu.roll(near, 1, 1)[:, 128:640]
        right = pltpu.roll(near, 767, 1)[:, 128:640]
        early = position[:, pl.ds(start, 512)]
        late = position[:, pl.ds(2 * CYCLE + start, 512)]
        angular = 4.0 * middle - left - right - early - late
        up = jnp.where(row == 0, above[:, pl.ds(start, 512)], pltpu.roll(middle, 1, 0))
        down = jnp.where(
            row == shells - 1, below[:, pl.ds(start, 512)], pltpu.roll(middle, shells - 1, 0)
        )
        radial = 2.0 * middle - up - down
        out[:, pl.ds(start, 512)] = -middle / square - ANGULAR * angular - RADIAL * radial
        some = counts[:, pl.ds(start, 512)].astype(jnp.float32)
        for lane in range(0, 512, 128):
            totals[...] += some[:, lane : lane + 128]
        return carry

    lax.fori_loop(0, pixels // 512, step, 0)


def stencil(field, momentum, before, after, above, below, scale, counts):
    shells, pixels = field.shape
    return pl.pallas_call(
        stencil_body,
        out_shape=[
            jax.ShapeDtypeStruct((shells, pixels), jnp.float32),
            jax.ShapeDtypeStruct((counts.shape[0], 128), jnp.float32),
        ],
        scratch_shapes=[pltpu.VMEM((shells, pixels + 2 * CYCLE), jnp.float32)],
        name="stencil",
    )(field, momentum, before, after, above, below, scale, counts)


def ratio_body(piece, own, partner, first, second, third, counts, mask, out, logs):
    rows, sub = out.shape
    total = jnp.zeros(logs.shape, jnp.float32)
    mask_row = mask[...]
    for start in range(0, sub, WIDE):
        here = slice(start, start + WIDE)
        proj = own[0, :, here] + partner[0, :, here]
        proj = proj + first[:, here] + second[:, here] + third[:, here]
        some = counts[:, here]
        out[:, here] = some / proj
        term = some * jnp.log(proj * packed_row(mask_row, here, sub, rows // 2))
        for lane in range(0, WIDE, 128):
            total = total + term[:, lane : lane + 128]
    logs[...] = total


def ratio(piece, own, partner, first, second, third, counts, mask):
    rows, sub = first.shape
    whole = pl.BlockSpec((rows, sub), lambda i, where: (0, 0))
    front = pl.BlockSpec((1, rows, sub), lambda i, where: (0, 0, 0))
    return pl.pallas_call(
        ratio_body,
        grid_spec=pltpu.PrefetchScalarGridSpec(
            num_scalar_prefetch=1,
            grid=(1,),
            in_specs=[
                front,
                front,
                whole,
                whole,
                whole,
                whole,
                pl.BlockSpec((1, 2 * sub), lambda i, where: (0, where[0])),
            ],
            out_specs=[whole, pl.BlockSpec((rows, 128), lambda i, where: (0, 0))],
        ),
        out_shape=[
            jax.ShapeDtypeStruct((rows, sub), jnp.float32),
            jax.ShapeDtypeStruct((rows, 128), jnp.float32),
        ],
        name="ratio",
    )(piece, own, partner, first, second, third, counts, mask)


def gradient_body(pieces, *refs, count, classes, bins, deep):
    quotients, refs = refs[:count], refs[count:]
    scale, density, rest, depth, mask, table = refs[:6]
    out, weights = refs[-2:]
    shells, width = out.shape
    sub = width // 2

    @pl.when(pl.program_id(0) == 0)
    def _():
        weights[...] = backward_weights(table[...], classes, bins, shells, deep)

    def piece(quotient):
        depth_row, mask_row = depth[...], mask[...]
        level = scale[...]
        for start in range(0, sub, WIDE):
            here = slice(start, start + WIDE)
            difference = quotient[:, here] - level * packed_row(mask_row, here, sub, bins)
            filler = jnp.zeros((deep - 2 * bins, WIDE), jnp.float32)
            high, low = split(jnp.concatenate([difference, filler], axis=0))
            every = jnp.dot(
                weights[...],
                jnp.concatenate([high, low, high], axis=0),
                preferred_element_type=jnp.float32,
            )
            for side in range(2):
                there = slice(start + side * sub, start + side * sub + WIDE)
                chosen = depth_row[:, there]
                base = side * classes * shells
                back = every[base : base + shells]
                for k in range(1, classes):
                    begin = base + k * shells
                    back = jnp.where(chosen == k, every[begin : begin + shells], back)
                out[:, there] = density[:, there] * back + rest[:, there]

    for k in range(count):
        pl.when(pl.program_id(0) == k)(functools.partial(piece, quotients[k]))


def gradient(pieces, quotients, scale, density, rest, depth, mask, table, previous, classes, bins):
    shells, pixels = rest.shape
    count = len(quotients)
    width = pixels // 8
    deep = -(-2 * bins // 16) * 16
    here = lambda i, where: (0, where[i])
    fixed = lambda i, where: (0, 0)
    operands = [pieces, *quotients, scale, density, rest, depth, mask, table]
    specs = [pl.BlockSpec(q.shape, fixed) for q in quotients] + [
        pl.BlockSpec(scale.shape, fixed),
        pl.BlockSpec((shells, width), lambda i, where: (0, i)),
        pl.BlockSpec((shells, width), here),
        pl.BlockSpec((1, width), here),
        pl.BlockSpec((1, width), here),
        pl.BlockSpec(table.shape, fixed),
    ]
    aliases = {}
    if previous is not None:
        aliases = {len(operands): 0}
        operands.append(previous)
        specs.append(pl.BlockSpec(memory_space=pl.ANY))
    return pl.pallas_call(
        functools.partial(gradient_body, count=count, classes=classes, bins=bins, deep=deep),
        grid_spec=pltpu.PrefetchScalarGridSpec(
            num_scalar_prefetch=1,
            grid=(count,),
            in_specs=specs,
            out_specs=pl.BlockSpec((shells, width), here),
            scratch_shapes=[pltpu.VMEM((2 * classes * shells, 3 * deep), jnp.bfloat16)],
        ),
        out_shape=jax.ShapeDtypeStruct((shells, pixels), jnp.float32),
        input_output_aliases=aliases,
        name="gradient",
    )(*operands)


def swap(values, axis, bit):
    count = lax.axis_size(axis)
    return lax.ppermute(values, axis, [(i, i ^ bit) for i in range(count)])


def along(values, step):
    count = lax.axis_size("shell")
    return lax.ppermute(values, "shell", [(i, (i + 2 * step) % count) for i in range(count)])


def halo(values, axis, step):
    count = lax.axis_size(axis)
    pairs = [(i, i + step) for i in range(count) if 0 <= i + step < count]
    return lax.ppermute(values, axis, pairs)


def shards(field, momentum, kernels, depth_class, counts, mask, mean_counts, shell_scale):
    shells, pixels = field.shape
    classes, bins, _ = kernels.shape
    total_pix = pixels * lax.axis_size("pix")
    width = pixels // 8
    place = lax.axis_index("shell")
    chip, core = place // 2, place % 2
    turn = (chip + jnp.arange(4, dtype=jnp.int32)) % 4
    kept, given = core * 4 + turn, (1 - core) * 4 + turn

    depth = depth_class.reshape(1, pixels)
    cover = mask.reshape(1, pixels)
    table = jnp.transpose(kernels, (0, 2, 1)).reshape(classes * shells, bins)

    proj_given, density_given, weighted_given = project(
        given, field, momentum, depth, cover, table, classes, bins
    )
    proj_partner = swap(proj_given, "shell", 1)
    proj_kept, density_kept, weighted_kept = project(
        kept, field, momentum, depth, cover, table, classes, bins
    )

    def ends(part):
        return field[part] + LEAP * momentum[part]

    after = halo(ends(jnp.s_[:, :CYCLE]), "pix", -1)
    before = halo(ends(jnp.s_[:, pixels - CYCLE :]), "pix", 1)
    below = halo(ends(jnp.s_[:1]), "shell", -1)
    above = halo(ends(jnp.s_[shells - 1 :]), "shell", 1)

    sums = [proj_kept[d] + proj_partner[d] for d in (1, 2, 3)]
    third = along(sums[2], 3)
    first = along(sums[0], 1)
    second = along(sums[1], 2)

    rest, totals = stencil(
        field, momentum, before, after, above, below, shell_scale[:, None], counts
    )
    own_counts = lax.dynamic_slice(counts, (0, kept[0] * width), (bins, width))
    own_counts = own_counts.reshape(bins, 2, width // 2).transpose(1, 0, 2)
    own_counts = own_counts.reshape(2 * bins, width // 2).astype(jnp.float32)

    weighted = weighted_given + weighted_kept
    weighted = jnp.sum(weighted[:bins] + weighted[bins:], axis=1)
    joint = jnp.concatenate([weighted, jnp.sum(totals, axis=1)])
    joint = jnp.where((jnp.arange(2 * bins) < bins) | (place == 0), joint, 0.0)
    for axis, bit in (("pix", 4), ("pix", 8), ("pix", 16)):
        joint = joint + swap(joint, axis, bit)

    quotient, logs = ratio(
        kept[:1], proj_kept, proj_partner, first, second, third, own_counts, cover
    )
    from_back = along(quotient, 1)
    from_front = along(quotient, 3)
    from_far = along(quotient, 2)
    mine = [quotient, from_front, from_far, from_back]
    theirs = [swap(q, "shell", 1) for q in mine]

    tail = jnp.sum(logs).reshape(1)
    joint = jnp.concatenate([joint, tail])
    for axis, bit in (("pix", 1), ("pix", 2), ("shell", 2), ("shell", 4), ("shell", 1)):
        joint = joint + swap(joint, axis, bit)
    weighted, total, tail = joint[:bins], joint[bins : 2 * bins], joint[2 * bins :]
    for axis, bit in (("pix", 4), ("pix", 8), ("pix", 16)):
        tail = tail + swap(tail, axis, bit)

    norm = weighted / total_pix
    level = total / (total_pix * norm)
    level = jnp.concatenate([level, level]).reshape(2 * bins, 1)

    out = gradient(
        kept, mine, level, density_kept, rest, depth, cover, table, None, classes, bins
    )
    out = gradient(
        given, theirs, level, density_given, rest, depth, cover, table, out, classes, bins
    )

    loglik = tail[0] + jnp.sum(
        total * jnp.log(mean_counts / norm) - mean_counts * (weighted / norm)
    )
    return out, loglik / (bins * total_pix)


def solution(mesh):
    placed = (
        P("shell", "pix"),
        P("shell", "pix"),
        P(None, None, "shell"),
        P("pix"),
        P(None, "pix"),
        P("pix"),
        P(),
        P("shell"),
    )
    return jax.shard_map(
        shards, mesh=mesh, in_specs=placed, out_specs=(P("shell", "pix"), P()), check_vma=False
    )
```

```python
import functools

import jax
import jax.numpy as jnp
from jax import lax
from jax.experimental import pallas as pl
from jax.experimental.pallas import tpu as pltpu
from jax.sharding import PartitionSpec as P


CYCLE = 2048
LEAP = 0.1
ANGULAR = 0.5
RADIAL = 0.5
WIDE = 256


def split(values):
    high = values.astype(jnp.bfloat16)
    low = (values - high.astype(jnp.float32)).astype(jnp.bfloat16)
    return high, low


def iota(shape, dim):
    return lax.broadcasted_iota(jnp.int32, shape, dim)


def dot_nt(a, b):
    return lax.dot_general(a, b, (((1,), (1,)), ((), ())), preferred_element_type=jnp.float32)


def forward_weights(table, classes, bins, shells):
    rows, cols = classes * 2 * bins, 6 * shells
    spread = (iota((rows, bins), 0) % bins == iota((rows, bins), 1)).astype(jnp.bfloat16)
    same_class = iota((rows, classes * shells), 0) // (2 * bins) == (
        iota((rows, classes * shells), 1) // shells
    )
    place = (iota((classes * shells, cols), 0) % shells == iota((classes * shells, cols), 1) % shells)
    place = place.astype(jnp.bfloat16)
    parts = []
    for part in split(table):
        wide = jnp.where(same_class, dot_nt(spread, part), 0.0).astype(jnp.bfloat16)
        parts.append(jnp.dot(wide, place, preferred_element_type=jnp.float32))
    row, col = iota((rows, cols), 0), iota((rows, cols), 1)
    picked = jnp.where(col // (2 * shells) == 2, parts[1], parts[0])
    same_sub = (row // bins) % 2 == (col // shells) % 2
    return jnp.where(same_sub, picked, 0.0).astype(jnp.bfloat16)


def backward_weights(table, classes, bins, shells, depth):
    half = classes * shells
    rows, cols = 2 * half, 3 * depth
    place = iota((bins, cols), 0) == (iota((bins, cols), 1) % depth) % bins
    place = place.astype(jnp.bfloat16)
    parts = []
    for part in split(table):
        once = jnp.dot(part, place, preferred_element_type=jnp.float32)
        parts.append(jnp.concatenate([once, once], axis=0))
    row, col = iota((rows, cols), 0), iota((rows, cols), 1)
    picked = jnp.where(col // depth == 2, parts[1], parts[0])
    same_sub = row // half == (col % depth) // bins
    return jnp.where(same_sub, picked, 0.0).astype(jnp.bfloat16)


def packed_row(row, start, width, bins):
    first = row[:, pl.ds(start, WIDE)]
    second = row[:, pl.ds(start + width, WIDE)]
    return jnp.where(iota((2 * bins, WIDE), 0) < bins, first, second)


def position_of():
    place = lax.axis_index("shell")
    return place // 2, place % 2


def offset_of(half, turn, chip, width):
    return pl.multiple_of((half * 4 + (chip + turn) % 4) * width, width)


def project_piece(
    d, base, field, momentum, depth, mask, weights, proj, density, position, weighted, classes, bins
):
    sub = field.shape[2] // 2
    total = jnp.zeros(weighted.shape, jnp.float32)
    for start in range(0, sub, WIDE):
        halves = []
        for begin in (start, start + sub):
            here = slice(begin, begin + WIDE)
            place = field[d, :, here] + LEAP * momentum[d, :, here]
            values = jnp.exp(place)
            position[d, :, here] = place
            density[d, :, here] = values
            halves.append(values)
        high, low = split(jnp.concatenate(halves, axis=0))
        every = jnp.dot(
            weights[...],
            jnp.concatenate([high, low, high], axis=0),
            preferred_element_type=jnp.float32,
        )
        chosen = packed_row(depth, base + start, sub, bins)
        picked = every[: 2 * bins]
        for k in range(1, classes):
            picked = jnp.where(chosen == k, every[2 * bins * k : 2 * bins * (k + 1)], picked)
        proj[d, :, start : start + WIDE] = picked
        scaled = picked * packed_row(mask, base + start, sub, bins)
        for lane in range(0, WIDE, 128):
            total = total + scaled[:, lane : lane + 128]
    weighted[...] += total


def project_given_body(
    field,
    momentum,
    depth,
    mask,
    table_away,
    proj,
    density,
    position,
    weighted,
    field_kept,
    momentum_kept,
    depth_here,
    mask_here,
    weights,
    field_given,
    momentum_given,
    stage,
    table,
    marks,
    classes,
    bins,
):
    _, shells, width = field_given.shape
    chip, core = position_of()
    copies = [
        pltpu.make_async_copy(depth, depth_here, marks.at[16]),
        pltpu.make_async_copy(mask, mask_here, marks.at[17]),
    ]
    load_table = pltpu.make_async_copy(table_away, table, marks.at[18])
    load_table.start()

    def fetch(half, d, source, target, mark):
        begin = offset_of(half, d, chip, width)
        return pltpu.make_async_copy(
            source.at[:, pl.ds(begin, width)], target.at[d], marks.at[mark]
        )

    for d in range(4):
        copies.append(fetch(1 - core, d, field, field_given, 2 * d))
        copies.append(fetch(1 - core, d, momentum, momentum_given, 2 * d + 1))
    for d in range(4):
        copies.append(fetch(core, d, field, field_kept, 8 + 2 * d))
        copies.append(fetch(core, d, momentum, momentum_kept, 9 + 2 * d))
    for copy in copies:
        copy.start()
    load_table.wait()
    weights[...] = forward_weights(table[...], classes, bins, shells)
    weighted[...] = jnp.zeros_like(weighted)
    copies[0].wait()
    copies[1].wait()
    for d in range(4):
        copies[2 + 2 * d].wait()
        copies[3 + 2 * d].wait()
        project_piece(
            d,
            offset_of(1 - core, d, chip, width),
            field_given,
            momentum_given,
            depth_here,
            mask_here,
            weights,
            proj,
            stage,
            position,
            weighted,
            classes,
            bins,
        )
        copies.append(
            pltpu.make_async_copy(stage.at[d], density.at[d], marks.at[19 + d])
        )
        copies[-1].start()
    for copy in copies[10:]:
        copy.wait()


def in_hbm(*values):
    return [pltpu.with_memory_space_constraint(v, pltpu.HBM) for v in values]


def in_vmem(*values):
    return [pltpu.with_memory_space_constraint(v, pltpu.VMEM) for v in values]


HERE = pl.BlockSpec(memory_space=pltpu.VMEM)
AWAY = pl.BlockSpec(memory_space=pltpu.HBM)


LIMIT = pltpu.CompilerParams(vmem_limit_bytes=16 << 20)


def vmem(*shape, dtype=jnp.float32):
    return pltpu.VMEM(shape, dtype)


def project_given(field, momentum, depth, mask, table, classes, bins):
    shells, pixels = field.shape
    width = pixels // 8
    outs = [
        vmem(4, 2 * bins, width // 2),
        pltpu.HBM((4, shells, width), jnp.float32),
        vmem(4, shells, width),
        vmem(2 * bins, 128),
        vmem(4, shells, width),
        vmem(4, shells, width),
        vmem(1, pixels, dtype=jnp.int32),
        vmem(1, pixels),
        vmem(classes * 2 * bins, 6 * shells, dtype=jnp.bfloat16),
    ]
    return pl.pallas_call(
        functools.partial(project_given_body, classes=classes, bins=bins),
        in_specs=[AWAY] * 5,
        out_specs=[HERE, AWAY] + [HERE] * (len(outs) - 2),
        out_shape=outs,
        scratch_shapes=[
            vmem(4, shells, width),
            vmem(4, shells, width),
            vmem(4, shells, width),
            vmem(*table.shape),
            pltpu.SemaphoreType.DMA((23,)),
        ],
        compiler_params=LIMIT,
        name="project_given",
    )(*in_hbm(field, momentum, depth, mask, table))


def project_kept_body(
    field,
    momentum,
    depth,
    mask,
    weights,
    before,
    proj,
    density,
    position,
    weighted,
    stage,
    marks,
    classes,
    bins,
):
    width = field.shape[2]
    chip, core = position_of()
    weighted[...] = before[...]
    copies = []
    for d in range(4):
        project_piece(
            d,
            offset_of(core, d, chip, width),
            field,
            momentum,
            depth,
            mask,
            weights,
            proj,
            stage,
            position,
            weighted,
            classes,
            bins,
        )
        copies.append(pltpu.make_async_copy(stage.at[d], density.at[d], marks.at[d]))
        copies[-1].start()
    for copy in copies:
        copy.wait()


def project_kept(field, momentum, depth, mask, weights, before, classes, bins):
    _, shells, width = field.shape
    outs = [
        vmem(4, 2 * bins, width // 2),
        pltpu.HBM((4, shells, width), jnp.float32),
        vmem(4, shells, width),
        vmem(2 * bins, 128),
    ]
    return pl.pallas_call(
        functools.partial(project_kept_body, classes=classes, bins=bins),
        in_specs=[HERE] * 6,
        out_specs=[HERE, AWAY, HERE, HERE],
        out_shape=outs,
        scratch_shapes=[vmem(4, shells, width), pltpu.SemaphoreType.DMA((4,))],
        compiler_params=LIMIT,
        name="project_kept",
    )(*in_vmem(field, momentum, depth, mask, weights, before))


def combine_body(kept, partner, given_place, kept_place, own, first, second, third, head, tail):
    chip, core = position_of()
    for d, out in enumerate((own, first, second, third)):
        out[...] = kept[d] + partner[d]
    front, back = (4 - chip) % 4, (7 - chip) % 4
    edge = given_place.shape[2] - CYCLE

    @pl.when(core == 0)
    def _():
        head[...] = kept_place[front, :, :CYCLE]
        tail[...] = given_place[back, :, edge:]

    @pl.when(core == 1)
    def _():
        head[...] = given_place[front, :, :CYCLE]
        tail[...] = kept_place[back, :, edge:]


def combine(kept, partner, given_place, kept_place):
    _, rows, sub = kept.shape
    shells = given_place.shape[1]
    outs = [vmem(rows, sub)] * 4 + [vmem(shells, CYCLE)] * 2
    return pl.pallas_call(
        combine_body,
        in_specs=[HERE] * 4,
        out_specs=[HERE] * 6,
        out_shape=outs,
        compiler_params=LIMIT,
        name="combine",
    )(*in_vmem(kept, partner, given_place, kept_place))


def column(row, count):
    width = row.shape[1]
    at = iota((count, width), 0) % width == iota((count, width), 1)
    wide = jnp.broadcast_to(row, (8, width))
    return exact_rows(wide, at.astype(jnp.bfloat16))[:, :1]


def tally_body(
    counts, after, table, scale, mean, totals, own, weights, square, means, here, marks, deep
):
    bins, pixels = here.shape
    shells = square.shape[0]
    chip, core = position_of()
    part = pixels // 8
    copies = []
    for i in range(8):
        piece = pl.ds(i * part, part)
        copies.append(
            pltpu.make_async_copy(counts.at[:, piece], here.at[:, piece], marks.at[i])
        )
        copies[-1].start()
    weights[...] = backward_weights(table[...], table.shape[0] // shells, bins, shells, deep)
    size = column(scale[...], shells)
    square[...] = jnp.broadcast_to(1.0 / (size * size), square.shape)
    means[...] = jnp.broadcast_to(column(mean[...], 2 * bins), means.shape)
    totals[...] = jnp.zeros_like(totals)
    for i in range(8):
        copies[i].wait()

        def step(j, carry):
            begin = pl.multiple_of(i * part + j * 512, 512)
            some = here[:, pl.ds(begin, 512)]
            return carry + (some[:, :128] + some[:, 128:256]) + (some[:, 256:384] + some[:, 384:])

        total = lax.fori_loop(0, part // 512, step, jnp.zeros((bins, 128), jnp.int32), unroll=2)
        totals[...] += total.astype(jnp.float32)
    base = offset_of(core, 0, chip, part)
    sub = part // 2
    for start in range(0, sub, 512):
        there = slice(start, start + 512)
        own[:bins, there] = here[:, pl.ds(base + start, 512)].astype(jnp.float32)
        own[bins:, there] = here[:, pl.ds(base + sub + start, 512)].astype(jnp.float32)


def tally(counts, after, table, scale, mean):
    bins, pixels = counts.shape
    shells = scale.shape[1]
    deep = -(-2 * bins // 16) * 16
    return pl.pallas_call(
        functools.partial(tally_body, deep=deep),
        in_specs=[AWAY, HERE, pl.BlockSpec(), pl.BlockSpec(), pl.BlockSpec()],
        out_specs=[HERE] * 5,
        out_shape=[
            vmem(bins, 128),
            vmem(2 * bins, pixels // 16),
            vmem(2 * table.shape[0], 3 * deep, dtype=jnp.bfloat16),
            vmem(shells, 128),
            vmem(2 * bins, 128),
        ],
        scratch_shapes=[vmem(bins, pixels, dtype=jnp.int32), pltpu.SemaphoreType.DMA((8,))],
        compiler_params=LIMIT,
        name="tally",
    )(*in_hbm(counts), *in_vmem(after), table, scale, mean)


def stencil_body(
    given, kept, before, after, scale, away, to_partner, to_side, position, out, marks
):
    _, shells, width = given.shape
    pixels = 8 * width
    chip, core = position_of()
    position[:, :CYCLE] = before[...]
    position[:, CYCLE + pixels :] = after[...]
    for d in range(4):
        for source, half in ((given, 1 - core), (kept, core)):
            base = offset_of(half, d, chip, width)
            for start in range(0, width, 1024):
                values = source[d, :, start : start + 1024]
                position[:, pl.ds(CYCLE + base + start, 1024)] = values
                first, last = values[:1], values[shells - 1 :]
                here = pl.ds(base + start, 1024)
                to_partner[:, here] = jnp.where(core == 0, last, first)
                to_side[:, here] = jnp.where(core == 0, first, last)
    inverse = jnp.concatenate([scale[...]] * 4, axis=1)
    row = iota((shells, 512), 0)

    def step(i, carry):
        start = pl.multiple_of(i * 512, 512)
        near = position[:, pl.ds(CYCLE + start - 128, 512 + 256)]
        middle = near[:, 128:640]
        left = pltpu.roll(near, 1, 1)[:, 128:640]
        right = pltpu.roll(near, 767, 1)[:, 128:640]
        early = position[:, pl.ds(start, 512)]
        late = position[:, pl.ds(2 * CYCLE + start, 512)]
        angular = 4.0 * middle - left - right - early - late
        up = jnp.where(row == 0, 0.0, pltpu.roll(middle, 1, 0))
        down = jnp.where(row == shells - 1, 0.0, pltpu.roll(middle, shells - 1, 0))
        radial = 2.0 * middle - up - down
        out[:, pl.ds(start, 512)] = -middle * inverse - ANGULAR * angular - RADIAL * radial
        return carry

    copies = []
    steps = pixels // 4096
    for i in range(8):
        lax.fori_loop(i * steps, (i + 1) * steps, step, 0, unroll=4)
        piece = pl.ds(i * steps * 512, steps * 512)
        copies.append(pltpu.make_async_copy(out.at[:, piece], away.at[:, piece], marks.at[i]))
        copies[-1].start()
    for copy in copies:
        copy.wait()


def stencil(given, kept, before, after, scale):
    _, shells, width = given.shape
    pixels = 8 * width
    return pl.pallas_call(
        stencil_body,
        in_specs=[HERE] * 5,
        out_specs=[AWAY, HERE, HERE],
        out_shape=[
            pltpu.HBM((shells, pixels), jnp.float32), vmem(1, pixels), vmem(1, pixels)
        ],
        scratch_shapes=[
            vmem(shells, pixels + 2 * CYCLE),
            vmem(shells, pixels),
            pltpu.SemaphoreType.DMA((8,)),
        ],
        compiler_params=LIMIT,
        name="stencil",
    )(*in_vmem(given, kept, before, after, scale))


def exact_rows(values, ones):
    total = 0.0
    for _ in range(3):
        part = values.astype(jnp.bfloat16)
        values = values - part.astype(jnp.float32)
        total = total + dot_nt(ones, part)
    return total


def ratio_body(
    own, first, second, third, counts, mask, weighted, totals, later, out, stats
):
    rows, sub = out.shape
    bins = rows // 2
    chip, core = position_of()
    base = offset_of(core, 0, chip, 2 * sub)
    logs = jnp.zeros((rows, 128), jnp.float32)
    for start in range(0, sub, WIDE):
        here = slice(start, start + WIDE)
        proj = own[:, here] + first[:, here] + second[:, here] + third[:, here]
        some = counts[:, here]
        out[:, here] = some / proj
        term = some * jnp.log(proj * packed_row(mask, base + start, sub, bins))
        for lane in range(0, WIDE, 128):
            logs = logs + term[:, lane : lane + 128]
    mine = jnp.where((chip == 0) & (core == 0), totals[...], 0.0)
    gap = jnp.zeros((128 - 2 * rows - bins, 128), jnp.float32)
    sums = jnp.concatenate(
        [weighted[...], logs, mine, gap], axis=0
    )
    row = exact_rows(sums, jnp.ones((8, 128), jnp.bfloat16))[:1]
    stats[...] = jnp.broadcast_to(row[:, None], stats.shape)


def ratio(own, first, second, third, counts, mask, weighted, totals, later, devices):
    return pl.pallas_call(
        ratio_body,
        in_specs=[HERE] * 9,
        out_specs=[HERE, HERE],
        out_shape=[vmem(*own.shape), vmem(devices, 1, 128)],
        compiler_params=LIMIT,
        name="ratio",
    )(*in_vmem(own, first, second, third, counts, mask, weighted, totals, later))


def reduce_body(gathered, mean, level, loglik, bins, total_pix):
    row = jnp.sum(gathered[...], axis=0)
    row = jnp.broadcast_to(row, (8, 128))
    at, lane = iota((2 * bins, 128), 0) % bins, iota((2 * bins, 128), 1)
    pick = jnp.where((lane < 2 * bins) & (lane % bins == at), 1.0, 0.0)
    weighted = exact_rows(row, pick.astype(jnp.bfloat16))[:, :1]
    pick = jnp.where(lane - 4 * bins == at, 1.0, 0.0)
    total = exact_rows(row, pick.astype(jnp.bfloat16))[:, :1]
    norm = weighted / total_pix
    level[...] = jnp.broadcast_to(total / (total_pix * norm), level.shape)
    average = mean[:, :1]
    terms = total * jnp.log(average / norm) - average * (weighted / norm)
    terms = jnp.where(iota(terms.shape, 0) < bins, terms, 0.0)
    lane = iota((8, 128), 1)
    logs = jnp.where((lane >= 2 * bins) & (lane < 4 * bins), row, 0.0)[:1]
    value = jnp.sum(terms, axis=0, keepdims=True) + jnp.sum(logs, axis=1, keepdims=True)
    loglik[...] = jnp.broadcast_to(value / (bins * total_pix), loglik.shape)


def gradient_body(*refs, classes, bins, total_pix, mine):
    quotients, refs = refs[:4], refs[4:]
    density_away, rest_away, depth, mask, weights, partner, side = refs[:7]
    density, rest, stage, marks = refs[-4:]
    _, shells, width = stage.shape
    sub = width // 2
    chip, core = position_of()
    half = core if mine else 1 - core
    loads = []
    for d in range(4):
        base = offset_of(half, d, chip, width)
        loads.append(
            (
                pltpu.make_async_copy(density_away.at[d], density.at[d], marks.at[4 + d]),
                pltpu.make_async_copy(
                    rest_away.at[:, pl.ds(base, width)], rest.at[d], marks.at[8 + d]
                ),
            )
        )
        for load in loads[-1]:
            load.start()
    if mine:
        gathered, mean, out, level, loglik = refs[7:12]
        reduce_body(gathered, mean, level, loglik, bins, total_pix)
    else:
        level, _, out = refs[7:10]
    row = iota((shells, WIDE), 0)
    beside_partner = (row == 0) & (core == 1) | (row == shells - 1) & (core == 0)
    outside = (row == 0) & (core == 0) | (row == shells - 1) & (core == 1)
    share = jnp.concatenate([level[...]] * (WIDE // 128), axis=1)
    filler = jnp.zeros((weights.shape[1] // 3 - 2 * bins, WIDE), jnp.float32)
    copies = []
    for d in range(4):
        base = offset_of(half, d, chip, width)
        for load in loads[d]:
            load.wait()
        for start in range(0, sub, WIDE):
            difference = quotients[d][:, start : start + WIDE]
            difference = difference - share * packed_row(mask, base + start, sub, bins)
            high, low = split(jnp.concatenate([difference, filler], axis=0))
            every = jnp.dot(
                weights[...],
                jnp.concatenate([high, low, high], axis=0),
                preferred_element_type=jnp.float32,
            )
            for k in range(2):
                here = slice(start + k * sub, start + k * sub + WIDE)
                away = pl.ds(base + (start + k * sub), WIDE)
                chosen = depth[:, away]
                begin = k * classes * shells
                back = every[begin : begin + shells]
                for c in range(1, classes):
                    begin += shells
                    back = jnp.where(chosen == c, every[begin : begin + shells], back)
                near = jnp.where(beside_partner, partner[:, away], 0.0)
                near = jnp.where(outside, side[:, away], near)
                stage[d, :, here] = density[d, :, here] * back + (rest[d, :, here] + RADIAL * near)
        copies.append(
            pltpu.make_async_copy(stage.at[d], out.at[:, pl.ds(base, width)], marks.at[d])
        )
        copies[-1].start()
    for copy in copies:
        copy.wait()


def gradient(
    quotients, density, rest, depth, mask, weights, partner, side, extra, previous,
    classes, bins, total_pix,
):
    shells, pixels = rest.shape
    width = pixels // 8
    mine = previous is None
    operands = in_vmem(*quotients) + in_hbm(density, rest)
    operands += in_vmem(depth, mask, weights, partner, side, *extra)
    specs = [HERE] * 4 + [AWAY] * 2 + [HERE] * (len(operands) - 6)
    outs, out_specs, aliases = [jax.ShapeDtypeStruct((shells, pixels), jnp.float32)], [AWAY], {}
    if mine:
        outs += [vmem(2 * bins, 128), jax.ShapeDtypeStruct((8, 128), jnp.float32)]
        out_specs += [HERE, pl.BlockSpec()]
    else:
        aliases = {len(operands): 0}
        operands.append(previous)
        specs.append(AWAY)
    return pl.pallas_call(
        functools.partial(
            gradient_body, classes=classes, bins=bins, total_pix=total_pix, mine=mine
        ),
        in_specs=specs,
        out_specs=out_specs,
        out_shape=outs,
        scratch_shapes=[
            vmem(4, shells, width),
            vmem(4, shells, width),
            vmem(4, shells, width),
            pltpu.SemaphoreType.DMA((12,)),
        ],
        input_output_aliases=aliases,
        compiler_params=LIMIT,
        name="gradient_kept" if mine else "gradient_given",
    )(*operands)


def swap(values):
    count = lax.axis_size("shell")
    return lax.ppermute(values, "shell", [(i, i ^ 1) for i in range(count)])


def beside(values):
    count = lax.axis_size("shell")
    pairs = [(i, i + 1) for i in range(1, count - 1, 2)]
    return lax.ppermute(values, "shell", pairs + [(b, a) for a, b in pairs])


def along(values, step):
    count = lax.axis_size("shell")
    return lax.ppermute(values, "shell", [(i, (i + 2 * step) % count) for i in range(count)])


def halo(values, axis, step):
    count = lax.axis_size(axis)
    pairs = [(i, i + step) for i in range(count) if 0 <= i + step < count]
    return lax.ppermute(values, axis, pairs)


def shards(field, momentum, kernels, depth_class, counts, mask, mean_counts, shell_scale):
    shells, pixels = field.shape
    classes, bins, _ = kernels.shape
    devices = lax.axis_size("pix") * lax.axis_size("shell")
    total_pix = pixels * lax.axis_size("pix")
    table = jnp.transpose(kernels, (0, 2, 1)).reshape(classes * shells, bins)

    given = project_given(
        field,
        momentum,
        depth_class.reshape(1, pixels),
        mask.reshape(1, pixels),
        table,
        classes,
        bins,
    )
    proj, density_given, place_given, weighted, field_kept, momentum_kept = given[:6]
    depth, cover, weights = given[6:]
    proj_partner = swap(proj)
    proj_kept, density_kept, place_kept, weighted = project_kept(
        field_kept, momentum_kept, depth, cover, weights, weighted, classes, bins
    )
    own, first, second, third, head, tail = combine(
        proj_kept, proj_partner, place_given, place_kept
    )
    second = along(second, 2)
    first = along(first, 1)
    third = along(third, 3)
    after = halo(head, "pix", -1)
    before = halo(tail, "pix", 1)
    totals, own_counts, weights, square, mean = tally(
        counts, head, table, shell_scale.reshape(1, shells), mean_counts.reshape(1, bins)
    )
    rest, to_partner, to_side = stencil(place_given, place_kept, before, after, square)
    partner_row = swap(to_partner)
    side_row = beside(to_side)
    quotient, stats = ratio(
        own, first, second, third, own_counts, cover, weighted, totals, to_side, devices
    )

    from_far = along(quotient, 2)
    from_back = along(quotient, 1)
    from_front = along(quotient, 3)
    gathered = lax.all_to_all(stats, ("pix", "shell"), 0, 0)
    mine = [quotient, from_front, from_far, from_back]
    theirs = [swap(q) for q in mine[1:]]
    theirs = [swap(quotient), *theirs]

    common = (rest, depth, cover, weights, partner_row, side_row)
    out, level, loglik = gradient(
        mine, density_kept, *common, (gathered, mean), None, classes, bins, total_pix
    )
    (out,) = gradient(
        theirs, density_given, *common, (level,), out, classes, bins, total_pix
    )
    return out, loglik[0, 0]


def solution(mesh):
    placed = (
        P("shell", "pix"),
        P("shell", "pix"),
        P(None, None, "shell"),
        P("pix"),
        P(None, "pix"),
        P("pix"),
        P(),
        P("shell"),
    )
    return jax.shard_map(
        shards,
        mesh=mesh,
        in_specs=placed,
        out_specs=(P("shell", "pix"), P()),
        check_vma=False,
    )
```

```python
import functools

import jax
import jax.numpy as jnp
from jax import lax
from jax.experimental import pallas as pl
from jax.experimental.pallas import tpu as pltpu
from jax.sharding import PartitionSpec as P


CYCLE = 2048
LEAP = 0.1
ANGULAR = 0.5
RADIAL = 0.5
WIDE = 256


def split(values):
    high = values.astype(jnp.bfloat16)
    low = (values - high.astype(jnp.float32)).astype(jnp.bfloat16)
    return high, low


def iota(shape, dim):
    return lax.broadcasted_iota(jnp.int32, shape, dim)


def dot_nt(a, b):
    return lax.dot_general(a, b, (((1,), (1,)), ((), ())), preferred_element_type=jnp.float32)


def forward_weights(table, classes, bins, shells):
    rows, cols = classes * 2 * bins, 6 * shells
    spread = (iota((rows, bins), 0) % bins == iota((rows, bins), 1)).astype(jnp.bfloat16)
    same_class = iota((rows, classes * shells), 0) // (2 * bins) == (
        iota((rows, classes * shells), 1) // shells
    )
    place = (iota((classes * shells, cols), 0) % shells == iota((classes * shells, cols), 1) % shells)
    place = place.astype(jnp.bfloat16)
    parts = []
    for part in split(table):
        wide = jnp.where(same_class, dot_nt(spread, part), 0.0).astype(jnp.bfloat16)
        parts.append(jnp.dot(wide, place, preferred_element_type=jnp.float32))
    row, col = iota((rows, cols), 0), iota((rows, cols), 1)
    picked = jnp.where(col // (2 * shells) == 2, parts[1], parts[0])
    same_sub = (row // bins) % 2 == (col // shells) % 2
    return jnp.where(same_sub, picked, 0.0).astype(jnp.bfloat16)


def backward_weights(table, classes, bins, shells, depth):
    half = classes * shells
    rows, cols = 2 * half, 3 * depth
    place = iota((bins, cols), 0) == (iota((bins, cols), 1) % depth) % bins
    place = place.astype(jnp.bfloat16)
    parts = []
    for part in split(table):
        once = jnp.dot(part, place, preferred_element_type=jnp.float32)
        parts.append(jnp.concatenate([once, once], axis=0))
    row, col = iota((rows, cols), 0), iota((rows, cols), 1)
    picked = jnp.where(col // depth == 2, parts[1], parts[0])
    same_sub = row // half == (col % depth) // bins
    return jnp.where(same_sub, picked, 0.0).astype(jnp.bfloat16)


def packed_row(row, start, width, bins):
    first = row[:, pl.ds(start, WIDE)]
    second = row[:, pl.ds(start + width, WIDE)]
    return jnp.where(iota((2 * bins, WIDE), 0) < bins, first, second)


def position_of():
    place = lax.axis_index("shell")
    return place // 2, place % 2


def offset_of(half, turn, chip, width):
    return pl.multiple_of((half * 4 + (chip + turn) % 4) * width, width)


def project_piece(
    d, base, field, momentum, depth, weights, proj, density, position, classes, bins
):
    sub = field.shape[2] // 2
    for start in range(0, sub, WIDE):
        halves = []
        for begin in (start, start + sub):
            here = slice(begin, begin + WIDE)
            place = field[d, :, here] + LEAP * momentum[d, :, here]
            values = jnp.exp(place)
            position[d, :, here] = place
            density[d, :, here] = values
            halves.append(values)
        high, low = split(jnp.concatenate(halves, axis=0))
        every = jnp.dot(
            weights[...],
            jnp.concatenate([high, low, high], axis=0),
            preferred_element_type=jnp.float32,
        )
        chosen = packed_row(depth, base + start, sub, bins)
        picked = every[: 2 * bins]
        for k in range(1, classes):
            picked = jnp.where(chosen == k, every[2 * bins * k : 2 * bins * (k + 1)], picked)
        proj[d, :, start : start + WIDE] = picked


def project_given_body(
    field,
    momentum,
    depth,
    mask,
    table_away,
    proj,
    density,
    position,
    field_kept,
    momentum_kept,
    depth_here,
    mask_here,
    weights,
    field_given,
    momentum_given,
    stage,
    table,
    marks,
    classes,
    bins,
):
    _, shells, width = field_given.shape
    chip, core = position_of()
    copies = [
        pltpu.make_async_copy(depth, depth_here, marks.at[16]),
        pltpu.make_async_copy(mask, mask_here, marks.at[17]),
    ]
    load_table = pltpu.make_async_copy(table_away, table, marks.at[18])
    load_table.start()

    def fetch(half, d, source, target, mark):
        begin = offset_of(half, d, chip, width)
        return pltpu.make_async_copy(
            source.at[:, pl.ds(begin, width)], target.at[d], marks.at[mark]
        )

    for d in range(4):
        copies.append(fetch(1 - core, d, field, field_given, 2 * d))
        copies.append(fetch(1 - core, d, momentum, momentum_given, 2 * d + 1))
    for d in range(4):
        copies.append(fetch(core, d, field, field_kept, 8 + 2 * d))
        copies.append(fetch(core, d, momentum, momentum_kept, 9 + 2 * d))
    for copy in copies:
        copy.start()
    load_table.wait()
    weights[...] = forward_weights(table[...], classes, bins, shells)
    copies[0].wait()
    copies[1].wait()
    for d in range(4):
        copies[2 + 2 * d].wait()
        copies[3 + 2 * d].wait()
        project_piece(
            d,
            offset_of(1 - core, d, chip, width),
            field_given,
            momentum_given,
            depth_here,
            weights,
            proj,
            stage,
            position,
            classes,
            bins,
        )
        copies.append(
            pltpu.make_async_copy(stage.at[d], density.at[d], marks.at[19 + d])
        )
        copies[-1].start()
    for copy in copies[10:]:
        copy.wait()


def in_hbm(*values):
    return [pltpu.with_memory_space_constraint(v, pltpu.HBM) for v in values]


def in_vmem(*values):
    return [pltpu.with_memory_space_constraint(v, pltpu.VMEM) for v in values]


HERE = pl.BlockSpec(memory_space=pltpu.VMEM)
AWAY = pl.BlockSpec(memory_space=pltpu.HBM)


LIMIT = pltpu.CompilerParams(vmem_limit_bytes=16 << 20)


def vmem(*shape, dtype=jnp.float32):
    return pltpu.VMEM(shape, dtype)


def project_given(field, momentum, depth, mask, table, classes, bins):
    shells, pixels = field.shape
    width = pixels // 8
    outs = [
        vmem(4, 2 * bins, width // 2),
        pltpu.HBM((4, shells, width), jnp.float32),
        vmem(4, shells, width),
        vmem(4, shells, width),
        vmem(4, shells, width),
        vmem(1, pixels, dtype=jnp.int32),
        vmem(1, pixels),
        vmem(classes * 2 * bins, 6 * shells, dtype=jnp.bfloat16),
    ]
    return pl.pallas_call(
        functools.partial(project_given_body, classes=classes, bins=bins),
        in_specs=[AWAY] * 5,
        out_specs=[HERE, AWAY] + [HERE] * (len(outs) - 2),
        out_shape=outs,
        scratch_shapes=[
            vmem(4, shells, width),
            vmem(4, shells, width),
            vmem(4, shells, width),
            vmem(*table.shape),
            pltpu.SemaphoreType.DMA((23,)),
        ],
        compiler_params=LIMIT,
        name="project_given",
    )(*in_hbm(field, momentum, depth, mask, table))


def project_kept_body(
    field, momentum, depth, weights, proj, density, position, stage, marks, classes, bins
):
    width = field.shape[2]
    chip, core = position_of()
    copies = []
    for d in range(4):
        project_piece(
            d,
            offset_of(core, d, chip, width),
            field,
            momentum,
            depth,
            weights,
            proj,
            stage,
            position,
            classes,
            bins,
        )
        copies.append(pltpu.make_async_copy(stage.at[d], density.at[d], marks.at[d]))
        copies[-1].start()
    for copy in copies:
        copy.wait()


def project_kept(field, momentum, depth, weights, classes, bins):
    _, shells, width = field.shape
    outs = [
        vmem(4, 2 * bins, width // 2),
        pltpu.HBM((4, shells, width), jnp.float32),
        vmem(4, shells, width),
    ]
    return pl.pallas_call(
        functools.partial(project_kept_body, classes=classes, bins=bins),
        in_specs=[HERE] * 4,
        out_specs=[HERE, AWAY, HERE],
        out_shape=outs,
        scratch_shapes=[vmem(4, shells, width), pltpu.SemaphoreType.DMA((4,))],
        compiler_params=LIMIT,
        name="project_kept",
    )(*in_vmem(field, momentum, depth, weights))


def combine_body(kept, partner, given_place, kept_place, own, first, second, third, head, tail):
    chip, core = position_of()
    for d, out in enumerate((own, first, second, third)):
        out[...] = kept[d] + partner[d]
    front, back = (4 - chip) % 4, (7 - chip) % 4
    edge = given_place.shape[2] - CYCLE

    @pl.when(core == 0)
    def _():
        head[...] = kept_place[front, :, :CYCLE]
        tail[...] = given_place[back, :, edge:]

    @pl.when(core == 1)
    def _():
        head[...] = given_place[front, :, :CYCLE]
        tail[...] = kept_place[back, :, edge:]


def combine(kept, partner, given_place, kept_place):
    _, rows, sub = kept.shape
    shells = given_place.shape[1]
    outs = [vmem(rows, sub)] * 4 + [vmem(shells, CYCLE)] * 2
    return pl.pallas_call(
        combine_body,
        in_specs=[HERE] * 4,
        out_specs=[HERE] * 6,
        out_shape=outs,
        compiler_params=LIMIT,
        name="combine",
    )(*in_vmem(kept, partner, given_place, kept_place))


def column(row, count):
    width = row.shape[1]
    at = iota((count, width), 0) % width == iota((count, width), 1)
    wide = jnp.broadcast_to(row, (8, width))
    return exact_rows(wide, at.astype(jnp.bfloat16))[:, :1]


def prepare_body(
    counts,
    given,
    kept,
    after,
    table,
    scale,
    mean,
    own,
    weights,
    square,
    means,
    kernels,
    to_partner,
    to_side,
    here,
    mark,
    deep,
):
    bins, part = here.shape
    shells = square.shape[0]
    chip, core = position_of()
    base = offset_of(core, 0, chip, part)
    copy = pltpu.make_async_copy(counts.at[:, pl.ds(base, part)], here, mark)
    copy.start()
    weights[...] = backward_weights(table[...], table.shape[0] // shells, bins, shells, deep)
    size = column(scale[...], shells)
    square[...] = jnp.broadcast_to(1.0 / (size * size), square.shape)
    means[...] = mean[...]
    kernels[...] = table[...]
    for d in range(4):
        for source, half in ((given, 1 - core), (kept, core)):
            begin = offset_of(half, d, chip, part)
            for start in range(0, part, 1024):
                first = source[d, :1, start : start + 1024]
                last = source[d, shells - 1 :, start : start + 1024]
                there = pl.ds(begin + start, 1024)
                to_partner[:, there] = jnp.where(core == 0, last, first)
                to_side[:, there] = jnp.where(core == 0, first, last)
    copy.wait()
    sub = part // 2
    for start in range(0, sub, 512):
        there = slice(start, start + 512)
        own[:bins, there] = here[:, there].astype(jnp.float32)
        own[bins:, there] = here[:, start + sub : start + sub + 512].astype(jnp.float32)


def prepare(counts, given, kept, after, table, scale, mean):
    bins, pixels = counts.shape
    shells = scale.shape[1]
    deep = -(-2 * bins // 16) * 16
    return pl.pallas_call(
        functools.partial(prepare_body, deep=deep),
        in_specs=[AWAY, HERE, HERE, HERE, pl.BlockSpec(), pl.BlockSpec(), pl.BlockSpec()],
        out_specs=[HERE] * 7,
        out_shape=[
            vmem(2 * bins, pixels // 16),
            vmem(2 * table.shape[0], 3 * deep, dtype=jnp.bfloat16),
            vmem(shells, 128),
            vmem(1, bins),
            vmem(*table.shape),
            vmem(1, pixels),
            vmem(1, pixels),
        ],
        scratch_shapes=[vmem(bins, pixels // 8, dtype=jnp.int32), pltpu.SemaphoreType.DMA],
        compiler_params=LIMIT,
        name="prepare",
    )(*in_hbm(counts), *in_vmem(given, kept, after), table, scale, mean)


def stencil_body(
    given, kept, before, after, scale, away, position, out, marks
):
    _, shells, width = given.shape
    pixels = 8 * width
    chip, core = position_of()
    position[:, :CYCLE] = before[...]
    position[:, CYCLE + pixels :] = after[...]
    for d in range(4):
        for source, half in ((given, 1 - core), (kept, core)):
            base = offset_of(half, d, chip, width)
            for start in range(0, width, 1024):
                values = source[d, :, start : start + 1024]
                position[:, pl.ds(CYCLE + base + start, 1024)] = values
    inverse = jnp.concatenate([scale[...]] * 4, axis=1)
    row = iota((shells, 512), 0)

    def step(i, carry):
        start = pl.multiple_of(i * 512, 512)
        near = position[:, pl.ds(CYCLE + start - 128, 512 + 256)]
        middle = near[:, 128:640]
        left = pltpu.roll(near, 1, 1)[:, 128:640]
        right = pltpu.roll(near, 767, 1)[:, 128:640]
        early = position[:, pl.ds(start, 512)]
        late = position[:, pl.ds(2 * CYCLE + start, 512)]
        angular = 4.0 * middle - left - right - early - late
        up = jnp.where(row == 0, 0.0, pltpu.roll(middle, 1, 0))
        down = jnp.where(row == shells - 1, 0.0, pltpu.roll(middle, shells - 1, 0))
        radial = 2.0 * middle - up - down
        out[:, pl.ds(start, 512)] = -middle * inverse - ANGULAR * angular - RADIAL * radial
        return carry

    copies = []
    steps = pixels // 4096
    for i in range(8):
        lax.fori_loop(i * steps, (i + 1) * steps, step, 0, unroll=4)
        piece = pl.ds(i * steps * 512, steps * 512)
        copies.append(pltpu.make_async_copy(out.at[:, piece], away.at[:, piece], marks.at[i]))
        copies[-1].start()
    for copy in copies:
        copy.wait()


def stencil(given, kept, before, after, scale):
    _, shells, width = given.shape
    pixels = 8 * width
    return pl.pallas_call(
        stencil_body,
        in_specs=[HERE] * 5,
        out_specs=AWAY,
        out_shape=pltpu.HBM((shells, pixels), jnp.float32),
        scratch_shapes=[
            vmem(shells, pixels + 2 * CYCLE),
            vmem(shells, pixels),
            pltpu.SemaphoreType.DMA((8,)),
        ],
        compiler_params=LIMIT,
        name="stencil",
    )(*in_vmem(given, kept, before, after, scale))


def exact_rows(values, ones):
    total = 0.0
    for _ in range(3):
        part = values.astype(jnp.bfloat16)
        values = values - part.astype(jnp.float32)
        total = total + dot_nt(ones, part)
    return total


def ratio_body(own, first, second, third, counts, mask, later, out, stats):
    rows, sub = out.shape
    bins = rows // 2
    chip, core = position_of()
    base = offset_of(core, 0, chip, 2 * sub)
    weighted = logs = totals = jnp.zeros((rows, 128), jnp.float32)
    for start in range(0, sub, WIDE):
        here = slice(start, start + WIDE)
        proj = own[:, here] + first[:, here] + second[:, here] + third[:, here]
        some = counts[:, here]
        out[:, here] = some / proj
        covered = proj * packed_row(mask, base + start, sub, bins)
        term = some * jnp.log(covered)
        for lane in range(0, WIDE, 128):
            weighted = weighted + covered[:, lane : lane + 128]
            logs = logs + term[:, lane : lane + 128]
            totals = totals + some[:, lane : lane + 128]
    filler = jnp.zeros((128 - 3 * rows, 128), jnp.float32)
    sums = jnp.concatenate([weighted, logs, totals, filler], axis=0)
    row = exact_rows(sums, jnp.ones((8, 128), jnp.bfloat16))[:1]
    stats[...] = jnp.broadcast_to(row[:, None], stats.shape)


def ratio(own, first, second, third, counts, mask, later):
    return pl.pallas_call(
        ratio_body,
        in_specs=[HERE] * 6 + [AWAY],
        out_specs=[HERE, HERE],
        out_shape=[
            vmem(*own.shape),
            vmem(lax.axis_size("pix") * lax.axis_size("shell"), 1, 128),
        ],
        compiler_params=LIMIT,
        name="ratio",
    )(*in_vmem(own, first, second, third, counts, mask), *in_hbm(later))


def lanes_of(row, low, high, bins):
    at, lane = iota((bins, 128), 0), iota((bins, 128), 1)
    pick = (lane >= low) & (lane < high) & (lane % bins == at)
    pick = jnp.where(pick, 1.0, 0.0).astype(jnp.bfloat16)
    total = 0.0
    for _ in range(3):
        part = row.astype(jnp.bfloat16)
        row = row - part.astype(jnp.float32)
        total = total + dot_nt(part, pick)
    return total


def finish_body(
    gathered,
    mean,
    table,
    depth,
    mask,
    kept,
    given,
    density_kept,
    density_given,
    out,
    loglik,
    density,
    stage,
    marks,
    classes,
    bins,
    total_pix,
):
    _, shells, width = kept.shape
    chip, core = position_of()
    pieces, copies = [], []
    for d in range(4):
        for k, (side, away, half) in enumerate(
            ((kept, density_kept, core), (given, density_given, 1 - core))
        ):
            pieces.append((side, d, offset_of(half, d, chip, width)))
            slot = 2 * d + k
            copies.append(pltpu.make_async_copy(away.at[d], density.at[slot], marks.at[slot]))
            copies[-1].start()
    row = jnp.broadcast_to(jnp.sum(gathered[...], axis=0), (8, 128))
    weighted = lanes_of(row, 0, 2 * bins, bins)[:1]
    total = lanes_of(row, 4 * bins, 6 * bins, bins)[:1]
    norm = weighted / total_pix
    level = total / (total_pix * norm)
    average = mean[...]
    terms = total * jnp.log(average / norm) - average * (weighted / norm)
    lane = iota((1, 128), 1)
    logs = jnp.where((lane >= 2 * bins) & (lane < 4 * bins), row[:1], 0.0)
    value = jnp.sum(terms, axis=1, keepdims=True) + jnp.sum(logs, axis=1, keepdims=True)
    loglik[...] = value / (bins * total_pix)
    drop = jnp.sum(table[...] * level, axis=1, keepdims=True)
    drop = jnp.broadcast_to(drop, (drop.shape[0], WIDE))
    for slot, (side, d, base) in enumerate(pieces):
        copies[slot].wait()
        for start in range(0, width, WIDE):
            here, away = slice(start, start + WIDE), pl.ds(base + start, WIDE)
            chosen = depth[:, away]
            less = drop[:shells]
            for c in range(1, classes):
                less = jnp.where(chosen == c, drop[c * shells : (c + 1) * shells], less)
            less = density[slot, :, here] * (mask[:, away] * less)
            stage[slot, :, here] = side[d, :, here] - less
        copies.append(
            pltpu.make_async_copy(
                stage.at[slot], out.at[:, pl.ds(base, width)], marks.at[8 + slot]
            )
        )
        copies[-1].start()
    for copy in copies[8:]:
        copy.wait()


def finish(
    gathered, mean, table, depth, mask, kept, given, density_kept, density_given, total_pix
):
    _, shells, width = kept.shape
    pixels, bins = 8 * width, table.shape[1]
    classes = table.shape[0] // shells
    operands = in_vmem(gathered, mean, table, depth, mask, kept, given)
    return pl.pallas_call(
        functools.partial(finish_body, classes=classes, bins=bins, total_pix=total_pix),
        in_specs=[HERE] * 7 + [AWAY] * 2,
        out_specs=[AWAY, pl.BlockSpec()],
        out_shape=[
            jax.ShapeDtypeStruct((shells, pixels), jnp.float32),
            jax.ShapeDtypeStruct((1, 1), jnp.float32),
        ],
        scratch_shapes=[
            vmem(8, shells, width),
            vmem(8, shells, width),
            pltpu.SemaphoreType.DMA((16,)),
        ],
        compiler_params=LIMIT,
        name="finish",
    )(*operands, *in_hbm(density_kept, density_given))


def gradient_body(*refs, classes, bins, mine):
    quotients, refs = refs[:4], refs[4:]
    density_away, rest_away, depth, weights, partner, side = refs[:6]
    out, density, rest, marks = refs[6:]
    _, shells, width = out.shape
    sub = width // 2
    chip, core = position_of()
    half = core if mine else 1 - core
    loads = []
    for d in range(4):
        base = offset_of(half, d, chip, width)
        loads.append(
            (
                pltpu.make_async_copy(density_away.at[d], density.at[d], marks.at[d]),
                pltpu.make_async_copy(
                    rest_away.at[:, pl.ds(base, width)], rest.at[d], marks.at[4 + d]
                ),
            )
        )
        for load in loads[-1]:
            load.start()
    row = iota((shells, WIDE), 0)
    beside_partner = (row == 0) & (core == 1) | (row == shells - 1) & (core == 0)
    outside = (row == 0) & (core == 0) | (row == shells - 1) & (core == 1)
    filler = jnp.zeros((weights.shape[1] // 3 - 2 * bins, WIDE), jnp.float32)
    for d in range(4):
        base = offset_of(half, d, chip, width)
        for load in loads[d]:
            load.wait()
        for start in range(0, sub, WIDE):
            values = quotients[d][:, start : start + WIDE]
            high, low = split(jnp.concatenate([values, filler], axis=0))
            every = jnp.dot(
                weights[...],
                jnp.concatenate([high, low, high], axis=0),
                preferred_element_type=jnp.float32,
            )
            for k in range(2):
                here = slice(start + k * sub, start + k * sub + WIDE)
                away = pl.ds(base + (start + k * sub), WIDE)
                chosen = depth[:, away]
                begin = k * classes * shells
                back = every[begin : begin + shells]
                for c in range(1, classes):
                    begin += shells
                    back = jnp.where(chosen == c, every[begin : begin + shells], back)
                near = jnp.where(beside_partner, partner[:, away], 0.0)
                near = jnp.where(outside, side[:, away], near)
                out[d, :, here] = density[d, :, here] * back + (rest[d, :, here] + RADIAL * near)


def gradient(quotients, density, rest, depth, weights, partner, side, classes, bins, mine):
    shells, pixels = rest.shape
    width = pixels // 8
    operands = in_vmem(*quotients) + in_hbm(density, rest)
    operands += in_vmem(depth, weights, partner, side)
    return pl.pallas_call(
        functools.partial(gradient_body, classes=classes, bins=bins, mine=mine),
        in_specs=[HERE] * 4 + [AWAY] * 2 + [HERE] * 4,
        out_specs=HERE,
        out_shape=vmem(4, shells, width),
        scratch_shapes=[
            vmem(4, shells, width),
            vmem(4, shells, width),
            pltpu.SemaphoreType.DMA((8,)),
        ],
        compiler_params=LIMIT,
        name="gradient_kept" if mine else "gradient_given",
    )(*operands)


def swap(values):
    count = lax.axis_size("shell")
    return lax.ppermute(values, "shell", [(i, i ^ 1) for i in range(count)])


def beside(values):
    count = lax.axis_size("shell")
    pairs = [(i, i + 1) for i in range(1, count - 1, 2)]
    return lax.ppermute(values, "shell", pairs + [(b, a) for a, b in pairs])


def along(values, step):
    count = lax.axis_size("shell")
    return lax.ppermute(values, "shell", [(i, (i + 2 * step) % count) for i in range(count)])


def halo(values, axis, step):
    count = lax.axis_size(axis)
    pairs = [(i, i + step) for i in range(count) if 0 <= i + step < count]
    return lax.ppermute(values, axis, pairs)


def shards(field, momentum, kernels, depth_class, counts, mask, mean_counts, shell_scale):
    shells, pixels = field.shape
    classes, bins, _ = kernels.shape
    total_pix = pixels * lax.axis_size("pix")
    table = jnp.transpose(kernels, (0, 2, 1)).reshape(classes * shells, bins)

    given = project_given(
        field,
        momentum,
        depth_class.reshape(1, pixels),
        mask.reshape(1, pixels),
        table,
        classes,
        bins,
    )
    proj, density_given, place_given, field_kept, momentum_kept, depth, cover, weights = given
    proj_partner = swap(proj)
    proj_kept, density_kept, place_kept = project_kept(
        field_kept, momentum_kept, depth, weights, classes, bins
    )
    own, first, second, third, head, tail = combine(
        proj_kept, proj_partner, place_given, place_kept
    )
    first = along(first, 1)
    third = along(third, 3)
    second = along(second, 2)
    after = halo(head, "pix", -1)
    before = halo(tail, "pix", 1)
    own_counts, weights, square, mean, table, to_partner, to_side = prepare(
        counts,
        place_given,
        place_kept,
        head,
        table,
        shell_scale.reshape(1, shells),
        mean_counts.reshape(1, bins),
    )
    partner_row = swap(to_partner)
    side_row = beside(to_side)
    rest = stencil(place_given, place_kept, before, after, square)
    quotient, stats = ratio(own, first, second, third, own_counts, cover, rest)
    from_back = along(quotient, 1)
    from_front = along(quotient, 3)
    from_far = along(quotient, 2)
    gathered = lax.all_to_all(stats, ("pix", "shell"), 0, 0)
    mine = [quotient, from_front, from_far, from_back]
    theirs = [swap(q) for q in mine[1:]]
    theirs = [swap(quotient), *theirs]

    common = (rest, depth, weights, partner_row, side_row, classes, bins)
    kept = gradient(mine, density_kept, *common, True)
    given = gradient(theirs, density_given, *common, False)
    out, loglik = finish(
        gathered, mean, table, depth, cover, kept, given, density_kept, density_given, total_pix
    )
    return out, loglik.reshape(())


def solution(mesh):
    placed = (
        P("shell", "pix"),
        P("shell", "pix"),
        P(None, None, "shell"),
        P("pix"),
        P(None, "pix"),
        P("pix"),
        P(),
        P("shell"),
    )
    return jax.shard_map(
        shards,
        mesh=mesh,
        in_specs=placed,
        out_specs=(P("shell", "pix"), P()),
        check_vma=False,
    )
```

```python
import functools

import jax
import jax.numpy as jnp
from jax import lax
from jax.experimental import pallas as pl
from jax.experimental.pallas import tpu as pltpu
from jax.sharding import PartitionSpec as P


CYCLE = 2048
LEAP = 0.1
ANGULAR = 0.5
RADIAL = 0.5
WIDE = 256


def split(values):
    high = values.astype(jnp.bfloat16)
    low = (values - high.astype(jnp.float32)).astype(jnp.bfloat16)
    return high, low


def iota(shape, dim):
    return lax.broadcasted_iota(jnp.int32, shape, dim)


def dot_nt(a, b):
    return lax.dot_general(a, b, (((1,), (1,)), ((), ())), preferred_element_type=jnp.float32)


def forward_weights(table, classes, bins, shells):
    rows, cols = classes * 2 * bins, 6 * shells
    spread = (iota((rows, bins), 0) % bins == iota((rows, bins), 1)).astype(jnp.bfloat16)
    same_class = iota((rows, classes * shells), 0) // (2 * bins) == (
        iota((rows, classes * shells), 1) // shells
    )
    place = (iota((classes * shells, cols), 0) % shells == iota((classes * shells, cols), 1) % shells)
    place = place.astype(jnp.bfloat16)
    parts = []
    for part in split(table):
        wide = jnp.where(same_class, dot_nt(spread, part), 0.0).astype(jnp.bfloat16)
        parts.append(jnp.dot(wide, place, preferred_element_type=jnp.float32))
    row, col = iota((rows, cols), 0), iota((rows, cols), 1)
    picked = jnp.where(col // (2 * shells) == 2, parts[1], parts[0])
    same_sub = (row // bins) % 2 == (col // shells) % 2
    return jnp.where(same_sub, picked, 0.0).astype(jnp.bfloat16)


def backward_weights(table, classes, bins, shells, depth):
    half = classes * shells
    rows, cols = 2 * half, 3 * depth
    place = iota((bins, cols), 0) == (iota((bins, cols), 1) % depth) % bins
    place = place.astype(jnp.bfloat16)
    parts = []
    for part in split(table):
        once = jnp.dot(part, place, preferred_element_type=jnp.float32)
        parts.append(jnp.concatenate([once, once], axis=0))
    row, col = iota((rows, cols), 0), iota((rows, cols), 1)
    picked = jnp.where(col // depth == 2, parts[1], parts[0])
    same_sub = row // half == (col % depth) // bins
    return jnp.where(same_sub, picked, 0.0).astype(jnp.bfloat16)


def packed_row(row, start, width, bins):
    first = row[:, pl.ds(start, WIDE)]
    second = row[:, pl.ds(start + width, WIDE)]
    return jnp.where(iota((2 * bins, WIDE), 0) < bins, first, second)


def position_of():
    place = lax.axis_index("shell")
    return place // 2, place % 2


def offset_of(half, turn, chip, width):
    return pl.multiple_of((half * 4 + (chip + turn) % 4) * width, width)


def project_piece(
    d, base, field, momentum, depth, weights, proj, density, position, classes, bins
):
    sub = field.shape[2] // 2
    for start in range(0, sub, WIDE):
        halves = []
        for begin in (start, start + sub):
            here = slice(begin, begin + WIDE)
            place = field[d, :, here] + LEAP * momentum[d, :, here]
            values = jnp.exp(place)
            position[d, :, here] = place
            density[d, :, here] = values
            halves.append(values)
        high, low = split(jnp.concatenate(halves, axis=0))
        every = jnp.dot(
            weights[...],
            jnp.concatenate([high, low, high], axis=0),
            preferred_element_type=jnp.float32,
        )
        chosen = packed_row(depth, base + start, sub, bins)
        picked = every[: 2 * bins]
        for k in range(1, classes):
            picked = jnp.where(chosen == k, every[2 * bins * k : 2 * bins * (k + 1)], picked)
        proj[d, :, start : start + WIDE] = picked


def project_given_body(
    field,
    momentum,
    depth,
    mask,
    table_away,
    proj,
    density,
    position,
    field_kept,
    momentum_kept,
    depth_here,
    mask_here,
    weights,
    field_given,
    momentum_given,
    stage,
    table,
    marks,
    classes,
    bins,
):
    _, shells, width = field_given.shape
    chip, core = position_of()
    copies = [
        pltpu.make_async_copy(depth, depth_here, marks.at[16]),
        pltpu.make_async_copy(mask, mask_here, marks.at[17]),
    ]
    load_table = pltpu.make_async_copy(table_away, table, marks.at[18])
    load_table.start()

    def fetch(half, d, source, target, mark):
        begin = offset_of(half, d, chip, width)
        return pltpu.make_async_copy(
            source.at[:, pl.ds(begin, width)], target.at[d], marks.at[mark]
        )

    for d in range(4):
        copies.append(fetch(1 - core, d, field, field_given, 2 * d))
        copies.append(fetch(1 - core, d, momentum, momentum_given, 2 * d + 1))
    for d in range(4):
        copies.append(fetch(core, d, field, field_kept, 8 + 2 * d))
        copies.append(fetch(core, d, momentum, momentum_kept, 9 + 2 * d))
    for copy in copies:
        copy.start()
    load_table.wait()
    weights[...] = forward_weights(table[...], classes, bins, shells)
    copies[0].wait()
    copies[1].wait()
    for d in range(4):
        copies[2 + 2 * d].wait()
        copies[3 + 2 * d].wait()
        project_piece(
            d,
            offset_of(1 - core, d, chip, width),
            field_given,
            momentum_given,
            depth_here,
            weights,
            proj,
            stage,
            position,
            classes,
            bins,
        )
        copies.append(
            pltpu.make_async_copy(stage.at[d], density.at[d], marks.at[19 + d])
        )
        copies[-1].start()
    for copy in copies[10:]:
        copy.wait()


def in_hbm(*values):
    return [pltpu.with_memory_space_constraint(v, pltpu.HBM) for v in values]


def in_vmem(*values):
    return [pltpu.with_memory_space_constraint(v, pltpu.VMEM) for v in values]


HERE = pl.BlockSpec(memory_space=pltpu.VMEM)
AWAY = pl.BlockSpec(memory_space=pltpu.HBM)


LIMIT = pltpu.CompilerParams(vmem_limit_bytes=16 << 20)


def vmem(*shape, dtype=jnp.float32):
    return pltpu.VMEM(shape, dtype)


def project_given(field, momentum, depth, mask, table, classes, bins):
    shells, pixels = field.shape
    width = pixels // 8
    outs = [
        vmem(4, 2 * bins, width // 2),
        pltpu.HBM((4, shells, width), jnp.float32),
        vmem(4, shells, width),
        vmem(4, shells, width),
        vmem(4, shells, width),
        vmem(1, pixels, dtype=jnp.int32),
        vmem(1, pixels),
        vmem(classes * 2 * bins, 6 * shells, dtype=jnp.bfloat16),
    ]
    return pl.pallas_call(
        functools.partial(project_given_body, classes=classes, bins=bins),
        in_specs=[AWAY] * 5,
        out_specs=[HERE, AWAY] + [HERE] * (len(outs) - 2),
        out_shape=outs,
        scratch_shapes=[
            vmem(4, shells, width),
            vmem(4, shells, width),
            vmem(4, shells, width),
            vmem(*table.shape),
            pltpu.SemaphoreType.DMA((23,)),
        ],
        compiler_params=LIMIT,
        name="project_given",
    )(*in_hbm(field, momentum, depth, mask, table))


def project_kept_body(
    field, momentum, depth, weights, proj, density, position, stage, marks, classes, bins
):
    width = field.shape[2]
    chip, core = position_of()
    copies = []
    for d in range(4):
        project_piece(
            d,
            offset_of(core, d, chip, width),
            field,
            momentum,
            depth,
            weights,
            proj,
            stage,
            position,
            classes,
            bins,
        )
        copies.append(pltpu.make_async_copy(stage.at[d], density.at[d], marks.at[d]))
        copies[-1].start()
    for copy in copies:
        copy.wait()


def project_kept(field, momentum, depth, weights, classes, bins):
    _, shells, width = field.shape
    outs = [
        vmem(4, 2 * bins, width // 2),
        pltpu.HBM((4, shells, width), jnp.float32),
        vmem(4, shells, width),
    ]
    return pl.pallas_call(
        functools.partial(project_kept_body, classes=classes, bins=bins),
        in_specs=[HERE] * 4,
        out_specs=[HERE, AWAY, HERE],
        out_shape=outs,
        scratch_shapes=[vmem(4, shells, width), pltpu.SemaphoreType.DMA((4,))],
        compiler_params=LIMIT,
        name="project_kept",
    )(*in_vmem(field, momentum, depth, weights))


def combine_body(kept, partner, given_place, kept_place, own, first, second, third, near, beyond):
    chip, core = position_of()
    for d, out in enumerate((own, first, second, third)):
        out[...] = kept[d] + partner[d]
    front, back = (4 - chip) % 4, (7 - chip) % 4
    edge = given_place.shape[2] - CYCLE
    even = lax.axis_index("pix") % 2 == 0

    def ends(low, high):
        head, tail = low[front, :, :CYCLE], high[back, :, edge:]
        near[...] = jnp.where(even, tail, head)
        beyond[...] = jnp.where(even, head, tail)

    pl.when(core == 0)(lambda: ends(kept_place, given_place))
    pl.when(core == 1)(lambda: ends(given_place, kept_place))


def combine(kept, partner, given_place, kept_place):
    _, rows, sub = kept.shape
    shells = given_place.shape[1]
    outs = [vmem(rows, sub)] * 4 + [vmem(shells, CYCLE)] * 2
    return pl.pallas_call(
        combine_body,
        in_specs=[HERE] * 4,
        out_specs=[HERE] * 6,
        out_shape=outs,
        compiler_params=LIMIT,
        name="combine",
    )(*in_vmem(kept, partner, given_place, kept_place))


def column(row, count):
    width = row.shape[1]
    at = iota((count, width), 0) % width == iota((count, width), 1)
    wide = jnp.broadcast_to(row, (8, width))
    return exact_rows(wide, at.astype(jnp.bfloat16))[:, :1]


def prepare_body(
    counts,
    given,
    kept,
    after,
    table,
    scale,
    mean,
    own,
    weights,
    square,
    means,
    kernels,
    to_partner,
    to_side,
    here,
    mark,
    deep,
):
    bins, part = here.shape
    shells = square.shape[0]
    chip, core = position_of()
    base = offset_of(core, 0, chip, part)
    copy = pltpu.make_async_copy(counts.at[:, pl.ds(base, part)], here, mark)
    copy.start()
    weights[...] = backward_weights(table[...], table.shape[0] // shells, bins, shells, deep)
    size = column(scale[...], shells)
    square[...] = jnp.broadcast_to(1.0 / (size * size), square.shape)
    means[...] = mean[...]
    kernels[...] = table[...]
    for d in range(4):
        for source, half in ((given, 1 - core), (kept, core)):
            begin = offset_of(half, d, chip, part)
            for start in range(0, part, 1024):
                first = source[d, :1, start : start + 1024]
                last = source[d, shells - 1 :, start : start + 1024]
                there = pl.ds(begin + start, 1024)
                to_partner[:, there] = jnp.where(core == 0, last, first)
                to_side[:, there] = jnp.where(core == 0, first, last)
    copy.wait()
    sub = part // 2
    for start in range(0, sub, 512):
        there = slice(start, start + 512)
        own[:bins, there] = here[:, there].astype(jnp.float32)
        own[bins:, there] = here[:, start + sub : start + sub + 512].astype(jnp.float32)


def prepare(counts, given, kept, after, table, scale, mean):
    bins, pixels = counts.shape
    shells = scale.shape[1]
    deep = -(-2 * bins // 16) * 16
    return pl.pallas_call(
        functools.partial(prepare_body, deep=deep),
        in_specs=[AWAY, HERE, HERE, HERE, pl.BlockSpec(), pl.BlockSpec(), pl.BlockSpec()],
        out_specs=[HERE] * 7,
        out_shape=[
            vmem(2 * bins, pixels // 16),
            vmem(2 * table.shape[0], 3 * deep, dtype=jnp.bfloat16),
            vmem(shells, 128),
            vmem(1, bins),
            vmem(*table.shape),
            vmem(1, pixels),
            vmem(1, pixels),
        ],
        scratch_shapes=[vmem(bins, pixels // 8, dtype=jnp.int32), pltpu.SemaphoreType.DMA],
        compiler_params=LIMIT,
        name="prepare",
    )(*in_hbm(counts), *in_vmem(given, kept, after), table, scale, mean)


def stencil_body(
    given, kept, near, beyond, scale, away, position, out, marks
):
    _, shells, width = given.shape
    pixels = 8 * width
    chip, core = position_of()
    even = lax.axis_index("pix") % 2 == 0
    position[:, :CYCLE] = jnp.where(even, beyond[...], near[...])
    position[:, CYCLE + pixels :] = jnp.where(even, near[...], beyond[...])
    for d in range(4):
        for source, half in ((given, 1 - core), (kept, core)):
            base = offset_of(half, d, chip, width)
            for start in range(0, width, 1024):
                values = source[d, :, start : start + 1024]
                position[:, pl.ds(CYCLE + base + start, 1024)] = values
    inverse = jnp.concatenate([scale[...]] * 4, axis=1)
    row = iota((shells, 512), 0)

    def step(i, carry):
        start = pl.multiple_of(i * 512, 512)
        near = position[:, pl.ds(CYCLE + start - 128, 512 + 256)]
        middle = near[:, 128:640]
        left = pltpu.roll(near, 1, 1)[:, 128:640]
        right = pltpu.roll(near, 767, 1)[:, 128:640]
        early = position[:, pl.ds(start, 512)]
        late = position[:, pl.ds(2 * CYCLE + start, 512)]
        angular = 4.0 * middle - left - right - early - late
        up = jnp.where(row == 0, 0.0, pltpu.roll(middle, 1, 0))
        down = jnp.where(row == shells - 1, 0.0, pltpu.roll(middle, shells - 1, 0))
        radial = 2.0 * middle - up - down
        out[:, pl.ds(start, 512)] = -middle * inverse - ANGULAR * angular - RADIAL * radial
        return carry

    copies = []
    steps = pixels // 4096
    for i in range(8):
        lax.fori_loop(i * steps, (i + 1) * steps, step, 0, unroll=4)
        piece = pl.ds(i * steps * 512, steps * 512)
        copies.append(pltpu.make_async_copy(out.at[:, piece], away.at[:, piece], marks.at[i]))
        copies[-1].start()
    for copy in copies:
        copy.wait()


def stencil(given, kept, before, after, scale):
    _, shells, width = given.shape
    pixels = 8 * width
    return pl.pallas_call(
        stencil_body,
        in_specs=[HERE] * 5,
        out_specs=AWAY,
        out_shape=pltpu.HBM((shells, pixels), jnp.float32),
        scratch_shapes=[
            vmem(shells, pixels + 2 * CYCLE),
            vmem(shells, pixels),
            pltpu.SemaphoreType.DMA((8,)),
        ],
        compiler_params=LIMIT,
        name="stencil",
    )(*in_vmem(given, kept, before, after, scale))


def exact_rows(values, ones):
    total = 0.0
    for _ in range(3):
        part = values.astype(jnp.bfloat16)
        values = values - part.astype(jnp.float32)
        total = total + dot_nt(ones, part)
    return total


def ratio_body(own, first, second, third, counts, mask, later, out, stats):
    rows, sub = out.shape
    bins = rows // 2
    chip, core = position_of()
    base = offset_of(core, 0, chip, 2 * sub)
    weighted = logs = totals = jnp.zeros((rows, 128), jnp.float32)
    for start in range(0, sub, WIDE):
        here = slice(start, start + WIDE)
        proj = own[:, here] + first[:, here] + second[:, here] + third[:, here]
        some = counts[:, here]
        out[:, here] = some / proj
        covered = proj * packed_row(mask, base + start, sub, bins)
        term = some * jnp.log(covered)
        for lane in range(0, WIDE, 128):
            weighted = weighted + covered[:, lane : lane + 128]
            logs = logs + term[:, lane : lane + 128]
            totals = totals + some[:, lane : lane + 128]
    filler = jnp.zeros((128 - 3 * rows, 128), jnp.float32)
    sums = jnp.concatenate([weighted, logs, totals, filler], axis=0)
    row = exact_rows(sums, jnp.ones((8, 128), jnp.bfloat16))[:1]
    stats[...] = jnp.broadcast_to(row[:, None], stats.shape)


def ratio(own, first, second, third, counts, mask, later):
    return pl.pallas_call(
        ratio_body,
        in_specs=[HERE] * 6 + [AWAY],
        out_specs=[HERE, HERE],
        out_shape=[
            vmem(*own.shape),
            vmem(lax.axis_size("pix") * lax.axis_size("shell"), 1, 128),
        ],
        compiler_params=LIMIT,
        name="ratio",
    )(*in_vmem(own, first, second, third, counts, mask), *in_hbm(later))


def lanes_of(row, low, high, bins):
    at, lane = iota((bins, 128), 0), iota((bins, 128), 1)
    pick = (lane >= low) & (lane < high) & (lane % bins == at)
    pick = jnp.where(pick, 1.0, 0.0).astype(jnp.bfloat16)
    total = 0.0
    for _ in range(3):
        part = row.astype(jnp.bfloat16)
        row = row - part.astype(jnp.float32)
        total = total + dot_nt(part, pick)
    return total


def finish_body(
    gathered,
    mean,
    table,
    depth,
    mask,
    kept,
    given,
    density_kept,
    density_given,
    out,
    loglik,
    density,
    stage,
    marks,
    classes,
    bins,
    total_pix,
):
    _, shells, width = kept.shape
    chip, core = position_of()
    pieces, copies = [], []
    for d in range(4):
        for k, (side, away, half) in enumerate(
            ((kept, density_kept, core), (given, density_given, 1 - core))
        ):
            pieces.append((side, d, offset_of(half, d, chip, width)))
            slot = 2 * d + k
            copies.append(pltpu.make_async_copy(away.at[d], density.at[slot], marks.at[slot]))
            copies[-1].start()
    row = jnp.broadcast_to(jnp.sum(gathered[...], axis=0), (8, 128))
    weighted = lanes_of(row, 0, 2 * bins, bins)[:1]
    total = lanes_of(row, 4 * bins, 6 * bins, bins)[:1]
    norm = weighted / total_pix
    level = total / (total_pix * norm)
    average = mean[...]
    terms = total * jnp.log(average / norm) - average * (weighted / norm)
    lane = iota((1, 128), 1)
    logs = jnp.where((lane >= 2 * bins) & (lane < 4 * bins), row[:1], 0.0)
    value = jnp.sum(terms, axis=1, keepdims=True) + jnp.sum(logs, axis=1, keepdims=True)
    loglik[...] = value / (bins * total_pix)
    drop = jnp.sum(table[...] * level, axis=1, keepdims=True)
    drop = jnp.broadcast_to(drop, (drop.shape[0], WIDE))
    for slot, (side, d, base) in enumerate(pieces):
        copies[slot].wait()
        for start in range(0, width, WIDE):
            here, away = slice(start, start + WIDE), pl.ds(base + start, WIDE)
            chosen = depth[:, away]
            less = drop[:shells]
            for c in range(1, classes):
                less = jnp.where(chosen == c, drop[c * shells : (c + 1) * shells], less)
            less = density[slot, :, here] * (mask[:, away] * less)
            stage[slot, :, here] = side[d, :, here] - less
        copies.append(
            pltpu.make_async_copy(
                stage.at[slot], out.at[:, pl.ds(base, width)], marks.at[8 + slot]
            )
        )
        copies[-1].start()
    for copy in copies[8:]:
        copy.wait()


def finish(
    gathered, mean, table, depth, mask, kept, given, density_kept, density_given, total_pix
):
    _, shells, width = kept.shape
    pixels, bins = 8 * width, table.shape[1]
    classes = table.shape[0] // shells
    operands = in_vmem(gathered, mean, table, depth, mask, kept, given)
    return pl.pallas_call(
        functools.partial(finish_body, classes=classes, bins=bins, total_pix=total_pix),
        in_specs=[HERE] * 7 + [AWAY] * 2,
        out_specs=[AWAY, pl.BlockSpec()],
        out_shape=[
            jax.ShapeDtypeStruct((shells, pixels), jnp.float32),
            jax.ShapeDtypeStruct((1, 1), jnp.float32),
        ],
        scratch_shapes=[
            vmem(8, shells, width),
            vmem(8, shells, width),
            pltpu.SemaphoreType.DMA((16,)),
        ],
        compiler_params=LIMIT,
        name="finish",
    )(*operands, *in_hbm(density_kept, density_given))


def gradient_body(*refs, classes, bins, mine):
    quotients, refs = refs[:4], refs[4:]
    density_away, rest_away, depth, weights, partner, side = refs[:6]
    out, density, rest, marks = refs[6:]
    _, shells, width = out.shape
    sub = width // 2
    chip, core = position_of()
    half = core if mine else 1 - core
    loads = []
    for d in range(4):
        base = offset_of(half, d, chip, width)
        loads.append(
            (
                pltpu.make_async_copy(density_away.at[d], density.at[d], marks.at[d]),
                pltpu.make_async_copy(
                    rest_away.at[:, pl.ds(base, width)], rest.at[d], marks.at[4 + d]
                ),
            )
        )
        for load in loads[-1]:
            load.start()
    row = iota((shells, WIDE), 0)
    beside_partner = (row == 0) & (core == 1) | (row == shells - 1) & (core == 0)
    outside = (row == 0) & (core == 0) | (row == shells - 1) & (core == 1)
    filler = jnp.zeros((weights.shape[1] // 3 - 2 * bins, WIDE), jnp.float32)
    for d in range(4):
        base = offset_of(half, d, chip, width)
        for load in loads[d]:
            load.wait()
        for start in range(0, sub, WIDE):
            values = quotients[d][:, start : start + WIDE]
            high, low = split(jnp.concatenate([values, filler], axis=0))
            every = jnp.dot(
                weights[...],
                jnp.concatenate([high, low, high], axis=0),
                preferred_element_type=jnp.float32,
            )
            for k in range(2):
                here = slice(start + k * sub, start + k * sub + WIDE)
                away = pl.ds(base + (start + k * sub), WIDE)
                chosen = depth[:, away]
                begin = k * classes * shells
                back = every[begin : begin + shells]
                for c in range(1, classes):
                    begin += shells
                    back = jnp.where(chosen == c, every[begin : begin + shells], back)
                near = jnp.where(beside_partner, partner[:, away], 0.0)
                near = jnp.where(outside, side[:, away], near)
                out[d, :, here] = density[d, :, here] * back + (rest[d, :, here] + RADIAL * near)


def gradient(quotients, density, rest, depth, weights, partner, side, classes, bins, mine):
    shells, pixels = rest.shape
    width = pixels // 8
    operands = in_vmem(*quotients) + in_hbm(density, rest)
    operands += in_vmem(depth, weights, partner, side)
    return pl.pallas_call(
        functools.partial(gradient_body, classes=classes, bins=bins, mine=mine),
        in_specs=[HERE] * 4 + [AWAY] * 2 + [HERE] * 4,
        out_specs=HERE,
        out_shape=vmem(4, shells, width),
        scratch_shapes=[
            vmem(4, shells, width),
            vmem(4, shells, width),
            pltpu.SemaphoreType.DMA((8,)),
        ],
        compiler_params=LIMIT,
        name="gradient_kept" if mine else "gradient_given",
    )(*operands)


def swap(values):
    count = lax.axis_size("shell")
    return lax.ppermute(values, "shell", [(i, i ^ 1) for i in range(count)])


def beside(values):
    count = lax.axis_size("shell")
    pairs = [(i, i + 1) for i in range(1, count - 1, 2)]
    return lax.ppermute(values, "shell", pairs + [(b, a) for a, b in pairs])


def along(values, step):
    count = lax.axis_size("shell")
    return lax.ppermute(values, "shell", [(i, (i + 2 * step) % count) for i in range(count)])


def across(values, start):
    pairs = [(i, i + 1) for i in range(start, lax.axis_size("pix") - 1, 2)]
    return lax.ppermute(values, "pix", pairs + [(b, a) for a, b in pairs])


def shards(field, momentum, kernels, depth_class, counts, mask, mean_counts, shell_scale):
    shells, pixels = field.shape
    classes, bins, _ = kernels.shape
    total_pix = pixels * lax.axis_size("pix")
    table = jnp.transpose(kernels, (0, 2, 1)).reshape(classes * shells, bins)

    given = project_given(
        field,
        momentum,
        depth_class.reshape(1, pixels),
        mask.reshape(1, pixels),
        table,
        classes,
        bins,
    )
    proj, density_given, place_given, field_kept, momentum_kept, depth, cover, weights = given
    proj_partner = swap(proj)
    proj_kept, density_kept, place_kept = project_kept(
        field_kept, momentum_kept, depth, weights, classes, bins
    )
    own, first, second, third, near, beyond = combine(
        proj_kept, proj_partner, place_given, place_kept
    )
    second = along(second, 2)
    first = along(first, 1)
    third = along(third, 3)
    near = across(near, 0)
    beyond = across(beyond, 1)
    own_counts, weights, square, mean, table, to_partner, to_side = prepare(
        counts,
        place_given,
        place_kept,
        own,
        table,
        shell_scale.reshape(1, shells),
        mean_counts.reshape(1, bins),
    )
    partner_row = swap(to_partner)
    side_row = beside(to_side)
    rest = stencil(place_given, place_kept, near, beyond, square)
    quotient, stats = ratio(own, first, second, third, own_counts, cover, rest)
    from_far = along(quotient, 2)
    from_back = along(quotient, 1)
    from_front = along(quotient, 3)
    gathered = lax.all_to_all(stats, ("pix", "shell"), 0, 0)
    mine = [quotient, from_front, from_far, from_back]
    theirs = [swap(q) for q in mine]

    common = (rest, depth, weights, partner_row, side_row, classes, bins)
    kept = gradient(mine, density_kept, *common, True)
    given = gradient(theirs, density_given, *common, False)
    out, loglik = finish(
        gathered, mean, table, depth, cover, kept, given, density_kept, density_given, total_pix
    )
    return out, loglik.reshape(())


def solution(mesh):
    placed = (
        P("shell", "pix"),
        P("shell", "pix"),
        P(None, None, "shell"),
        P("pix"),
        P(None, "pix"),
        P("pix"),
        P(),
        P("shell"),
    )
    return jax.shard_map(
        shards,
        mesh=mesh,
        in_specs=placed,
        out_specs=(P("shell", "pix"), P()),
        check_vma=False,
    )
```

```python
import functools

import jax
import jax.numpy as jnp
from jax import lax
from jax.experimental import pallas as pl
from jax.experimental.pallas import tpu as pltpu
from jax.sharding import Mesh, PartitionSpec as P


CYCLE = 2048
LEAP = 0.1
ANGULAR = 0.5
RADIAL = 0.5
WIDE = 256


def split(values):
    high = values.astype(jnp.bfloat16)
    low = (values - high.astype(jnp.float32)).astype(jnp.bfloat16)
    return high, low


def iota(shape, dim):
    return lax.broadcasted_iota(jnp.int32, shape, dim)


def dot_nt(a, b):
    return lax.dot_general(a, b, (((1,), (1,)), ((), ())), preferred_element_type=jnp.float32)


def forward_weights(table, classes, bins, shells):
    rows, cols = classes * 2 * bins, 6 * shells
    spread = (iota((rows, bins), 0) % bins == iota((rows, bins), 1)).astype(jnp.bfloat16)
    same_class = iota((rows, classes * shells), 0) // (2 * bins) == (
        iota((rows, classes * shells), 1) // shells
    )
    place = (iota((classes * shells, cols), 0) % shells == iota((classes * shells, cols), 1) % shells)
    place = place.astype(jnp.bfloat16)
    parts = []
    for part in split(table):
        wide = jnp.where(same_class, dot_nt(spread, part), 0.0).astype(jnp.bfloat16)
        parts.append(jnp.dot(wide, place, preferred_element_type=jnp.float32))
    row, col = iota((rows, cols), 0), iota((rows, cols), 1)
    picked = jnp.where(col // (2 * shells) == 2, parts[1], parts[0])
    same_sub = (row // bins) % 2 == (col // shells) % 2
    return jnp.where(same_sub, picked, 0.0).astype(jnp.bfloat16)


def backward_weights(table, classes, bins, shells, depth):
    half = classes * shells
    rows, cols = 2 * half, 3 * depth
    place = iota((bins, cols), 0) == (iota((bins, cols), 1) % depth) % bins
    place = place.astype(jnp.bfloat16)
    parts = []
    for part in split(table):
        once = jnp.dot(part, place, preferred_element_type=jnp.float32)
        parts.append(jnp.concatenate([once, once], axis=0))
    row, col = iota((rows, cols), 0), iota((rows, cols), 1)
    picked = jnp.where(col // depth == 2, parts[1], parts[0])
    same_sub = row // half == (col % depth) // bins
    return jnp.where(same_sub, picked, 0.0).astype(jnp.bfloat16)


def packed_row(row, start, width, bins):
    first = row[:, pl.ds(start, WIDE)]
    second = row[:, pl.ds(start + width, WIDE)]
    return jnp.where(iota((2 * bins, WIDE), 0) < bins, first, second)


def position_of():
    return lax.axis_index("x"), lax.axis_index("core")


def offset_of(half, turn, chip, width):
    return pl.multiple_of((half * 4 + (chip + turn) % 4) * width, width)


def project_piece(
    d, base, field, momentum, depth, weights, proj, density, position, classes, bins
):
    sub = field.shape[2] // 2
    for start in range(0, sub, WIDE):
        halves = []
        for begin in (start, start + sub):
            here = slice(begin, begin + WIDE)
            place = field[d, :, here] + LEAP * momentum[d, :, here]
            values = jnp.exp(place)
            position[d, :, here] = place
            density[d, :, here] = values
            halves.append(values)
        high, low = split(jnp.concatenate(halves, axis=0))
        every = jnp.dot(
            weights[...],
            jnp.concatenate([high, low, high], axis=0),
            preferred_element_type=jnp.float32,
        )
        chosen = packed_row(depth, base + start, sub, bins)
        picked = every[: 2 * bins]
        for k in range(1, classes):
            picked = jnp.where(chosen == k, every[2 * bins * k : 2 * bins * (k + 1)], picked)
        proj[d, :, start : start + WIDE] = picked


def project_given_body(
    field,
    momentum,
    depth,
    mask,
    table_away,
    proj,
    density,
    position,
    field_kept,
    momentum_kept,
    depth_here,
    mask_here,
    weights,
    field_given,
    momentum_given,
    stage,
    table,
    marks,
    classes,
    bins,
):
    _, shells, width = field_given.shape
    chip, core = position_of()
    copies = [
        pltpu.make_async_copy(depth, depth_here, marks.at[16]),
        pltpu.make_async_copy(mask, mask_here, marks.at[17]),
    ]
    load_table = pltpu.make_async_copy(table_away, table, marks.at[18])
    load_table.start()

    def fetch(half, d, source, target, mark):
        begin = offset_of(half, d, chip, width)
        return pltpu.make_async_copy(
            source.at[:, pl.ds(begin, width)], target.at[d], marks.at[mark]
        )

    for d in range(4):
        copies.append(fetch(1 - core, d, field, field_given, 2 * d))
        copies.append(fetch(1 - core, d, momentum, momentum_given, 2 * d + 1))
    for d in range(4):
        copies.append(fetch(core, d, field, field_kept, 8 + 2 * d))
        copies.append(fetch(core, d, momentum, momentum_kept, 9 + 2 * d))
    for copy in copies:
        copy.start()
    load_table.wait()
    weights[...] = forward_weights(table[...], classes, bins, shells)
    copies[0].wait()
    copies[1].wait()
    for d in range(4):
        copies[2 + 2 * d].wait()
        copies[3 + 2 * d].wait()
        project_piece(
            d,
            offset_of(1 - core, d, chip, width),
            field_given,
            momentum_given,
            depth_here,
            weights,
            proj,
            stage,
            position,
            classes,
            bins,
        )
        copies.append(
            pltpu.make_async_copy(stage.at[d], density.at[d], marks.at[19 + d])
        )
        copies[-1].start()
    for copy in copies[10:]:
        copy.wait()


def in_hbm(*values):
    return [pltpu.with_memory_space_constraint(v, pltpu.HBM) for v in values]


def in_vmem(*values):
    return [pltpu.with_memory_space_constraint(v, pltpu.VMEM) for v in values]


HERE = pl.BlockSpec(memory_space=pltpu.VMEM)
AWAY = pl.BlockSpec(memory_space=pltpu.HBM)


LIMIT = pltpu.CompilerParams(vmem_limit_bytes=16 << 20)


def vmem(*shape, dtype=jnp.float32):
    return pltpu.VMEM(shape, dtype)


def project_given(field, momentum, depth, mask, table, classes, bins):
    shells, pixels = field.shape
    width = pixels // 8
    outs = [
        vmem(4, 2 * bins, width // 2),
        pltpu.HBM((4, shells, width), jnp.float32),
        vmem(4, shells, width),
        vmem(4, shells, width),
        vmem(4, shells, width),
        vmem(1, pixels, dtype=jnp.int32),
        vmem(1, pixels),
        vmem(classes * 2 * bins, 6 * shells, dtype=jnp.bfloat16),
    ]
    return pl.pallas_call(
        functools.partial(project_given_body, classes=classes, bins=bins),
        in_specs=[AWAY] * 5,
        out_specs=[HERE, AWAY] + [HERE] * (len(outs) - 2),
        out_shape=outs,
        scratch_shapes=[
            vmem(4, shells, width),
            vmem(4, shells, width),
            vmem(4, shells, width),
            vmem(*table.shape),
            pltpu.SemaphoreType.DMA((23,)),
        ],
        compiler_params=LIMIT,
        name="project_given",
    )(*in_hbm(field, momentum, depth, mask, table))


def project_kept_body(
    field, momentum, depth, weights, proj, density, position, stage, marks, classes, bins
):
    width = field.shape[2]
    chip, core = position_of()
    copies = []
    for d in range(4):
        project_piece(
            d,
            offset_of(core, d, chip, width),
            field,
            momentum,
            depth,
            weights,
            proj,
            stage,
            position,
            classes,
            bins,
        )
        copies.append(pltpu.make_async_copy(stage.at[d], density.at[d], marks.at[d]))
        copies[-1].start()
    for copy in copies:
        copy.wait()


def project_kept(field, momentum, depth, weights, classes, bins):
    _, shells, width = field.shape
    outs = [
        vmem(4, 2 * bins, width // 2),
        pltpu.HBM((4, shells, width), jnp.float32),
        vmem(4, shells, width),
    ]
    return pl.pallas_call(
        functools.partial(project_kept_body, classes=classes, bins=bins),
        in_specs=[HERE] * 4,
        out_specs=[HERE, AWAY, HERE],
        out_shape=outs,
        scratch_shapes=[vmem(4, shells, width), pltpu.SemaphoreType.DMA((4,))],
        compiler_params=LIMIT,
        name="project_kept",
    )(*in_vmem(field, momentum, depth, weights))


def combine_body(kept, partner, given_place, kept_place, own, first, second, third, near, beyond):
    chip, core = position_of()
    for d, out in enumerate((own, first, second, third)):
        out[...] = kept[d] + partner[d]
    front, back = (4 - chip) % 4, (7 - chip) % 4
    edge = given_place.shape[2] - CYCLE
    even = lax.axis_index("pix") % 2 == 0

    def ends(low, high):
        head, tail = low[front, :, :CYCLE], high[back, :, edge:]
        near[...] = jnp.where(even, tail, head)
        beyond[...] = jnp.where(even, head, tail)

    pl.when(core == 0)(lambda: ends(kept_place, given_place))
    pl.when(core == 1)(lambda: ends(given_place, kept_place))


def combine(kept, partner, given_place, kept_place):
    _, rows, sub = kept.shape
    shells = given_place.shape[1]
    outs = [vmem(rows, sub)] * 4 + [vmem(shells, CYCLE)] * 2
    return pl.pallas_call(
        combine_body,
        in_specs=[HERE] * 4,
        out_specs=[HERE] * 6,
        out_shape=outs,
        compiler_params=LIMIT,
        name="combine",
    )(*in_vmem(kept, partner, given_place, kept_place))


def column(row, count):
    width = row.shape[1]
    at = iota((count, width), 0) % width == iota((count, width), 1)
    wide = jnp.broadcast_to(row, (8, width))
    return exact_rows(wide, at.astype(jnp.bfloat16))[:, :1]


def prepare_body(
    counts,
    given,
    kept,
    after,
    table,
    scale,
    mean,
    own,
    weights,
    square,
    means,
    kernels,
    to_partner,
    to_side,
    here,
    mark,
    deep,
):
    bins, part = here.shape
    shells = square.shape[0]
    chip, core = position_of()
    base = offset_of(core, 0, chip, part)
    copy = pltpu.make_async_copy(counts.at[:, pl.ds(base, part)], here, mark)
    copy.start()
    weights[...] = backward_weights(table[...], table.shape[0] // shells, bins, shells, deep)
    size = column(scale[...], shells)
    square[...] = jnp.broadcast_to(1.0 / (size * size), square.shape)
    means[...] = mean[...]
    kernels[...] = table[...]
    for d in range(4):
        for source, half in ((given, 1 - core), (kept, core)):
            begin = offset_of(half, d, chip, part)
            for start in range(0, part, 1024):
                first = source[d, :1, start : start + 1024]
                last = source[d, shells - 1 :, start : start + 1024]
                there = pl.ds(begin + start, 1024)
                to_partner[:, there] = jnp.where(core == 0, last, first)
                to_side[:, there] = jnp.where(core == 0, first, last)
    copy.wait()
    sub = part // 2
    for start in range(0, sub, 512):
        there = slice(start, start + 512)
        own[:bins, there] = here[:, there].astype(jnp.float32)
        own[bins:, there] = here[:, start + sub : start + sub + 512].astype(jnp.float32)


def prepare(counts, given, kept, after, table, scale, mean):
    bins, pixels = counts.shape
    shells = scale.shape[1]
    deep = -(-2 * bins // 16) * 16
    return pl.pallas_call(
        functools.partial(prepare_body, deep=deep),
        in_specs=[AWAY, HERE, HERE, HERE, pl.BlockSpec(), pl.BlockSpec(), pl.BlockSpec()],
        out_specs=[HERE] * 7,
        out_shape=[
            vmem(2 * bins, pixels // 16),
            vmem(2 * table.shape[0], 3 * deep, dtype=jnp.bfloat16),
            vmem(shells, 128),
            vmem(1, bins),
            vmem(*table.shape),
            vmem(1, pixels),
            vmem(1, pixels),
        ],
        scratch_shapes=[vmem(bins, pixels // 8, dtype=jnp.int32), pltpu.SemaphoreType.DMA],
        compiler_params=LIMIT,
        name="prepare",
    )(*in_hbm(counts), *in_vmem(given, kept, after), table, scale, mean)


def stencil_body(
    given, kept, near, beyond, scale, away, position, out, marks
):
    _, shells, width = given.shape
    pixels = 8 * width
    chip, core = position_of()
    even = lax.axis_index("pix") % 2 == 0
    position[:, :CYCLE] = jnp.where(even, beyond[...], near[...])
    position[:, CYCLE + pixels :] = jnp.where(even, near[...], beyond[...])
    for d in range(4):
        for source, half in ((given, 1 - core), (kept, core)):
            base = offset_of(half, d, chip, width)
            for start in range(0, width, 1024):
                values = source[d, :, start : start + 1024]
                position[:, pl.ds(CYCLE + base + start, 1024)] = values
    inverse = jnp.concatenate([scale[...]] * 4, axis=1)
    row = iota((shells, 512), 0)

    def step(i, carry):
        start = pl.multiple_of(i * 512, 512)
        near = position[:, pl.ds(CYCLE + start - 128, 512 + 256)]
        middle = near[:, 128:640]
        left = pltpu.roll(near, 1, 1)[:, 128:640]
        right = pltpu.roll(near, 767, 1)[:, 128:640]
        early = position[:, pl.ds(start, 512)]
        late = position[:, pl.ds(2 * CYCLE + start, 512)]
        angular = 4.0 * middle - left - right - early - late
        up = jnp.where(row == 0, 0.0, pltpu.roll(middle, 1, 0))
        down = jnp.where(row == shells - 1, 0.0, pltpu.roll(middle, shells - 1, 0))
        radial = 2.0 * middle - up - down
        out[:, pl.ds(start, 512)] = -middle * inverse - ANGULAR * angular - RADIAL * radial
        return carry

    copies = []
    steps = pixels // 4096
    for i in range(8):
        lax.fori_loop(i * steps, (i + 1) * steps, step, 0, unroll=4)
        piece = pl.ds(i * steps * 512, steps * 512)
        copies.append(pltpu.make_async_copy(out.at[:, piece], away.at[:, piece], marks.at[i]))
        copies[-1].start()
    for copy in copies:
        copy.wait()


def stencil(given, kept, before, after, scale):
    _, shells, width = given.shape
    pixels = 8 * width
    return pl.pallas_call(
        stencil_body,
        in_specs=[HERE] * 5,
        out_specs=AWAY,
        out_shape=pltpu.HBM((shells, pixels), jnp.float32),
        scratch_shapes=[
            vmem(shells, pixels + 2 * CYCLE),
            vmem(shells, pixels),
            pltpu.SemaphoreType.DMA((8,)),
        ],
        compiler_params=LIMIT,
        name="stencil",
    )(*in_vmem(given, kept, before, after, scale))


def exact_rows(values, ones):
    total = 0.0
    for _ in range(3):
        part = values.astype(jnp.bfloat16)
        values = values - part.astype(jnp.float32)
        total = total + dot_nt(ones, part)
    return total


def ratio_body(own, first, second, third, counts, mask, later, out, stats):
    rows, sub = out.shape
    bins = rows // 2
    chip, core = position_of()
    base = offset_of(core, 0, chip, 2 * sub)
    weighted = logs = totals = jnp.zeros((rows, 128), jnp.float32)
    for start in range(0, sub, WIDE):
        here = slice(start, start + WIDE)
        proj = own[:, here] + first[:, here] + second[:, here] + third[:, here]
        some = counts[:, here]
        out[:, here] = some / proj
        covered = proj * packed_row(mask, base + start, sub, bins)
        term = some * jnp.log(covered)
        for lane in range(0, WIDE, 128):
            weighted = weighted + covered[:, lane : lane + 128]
            logs = logs + term[:, lane : lane + 128]
            totals = totals + some[:, lane : lane + 128]
    gap = jnp.zeros((32 - bins, 128), jnp.float32)
    sums = jnp.concatenate(
        [
            weighted[:bins] + weighted[bins:],
            gap,
            totals[:bins] + totals[bins:],
            gap,
            logs,
            jnp.zeros((64 - rows, 128), jnp.float32),
        ],
        axis=0,
    )
    row = exact_rows(sums, jnp.ones((8, 128), jnp.bfloat16))[:1]
    stats[...] = jnp.broadcast_to(row.reshape((1,) * (stats.ndim - 1) + (128,)), stats.shape)


def ratio(own, first, second, third, counts, mask, later):
    return pl.pallas_call(
        ratio_body,
        in_specs=[HERE] * 6 + [AWAY],
        out_specs=[HERE, HERE],
        out_shape=[
            vmem(*own.shape),
            vmem(1, 128),
        ],
        compiler_params=LIMIT,
        name="ratio",
    )(*in_vmem(own, first, second, third, counts, mask), *in_hbm(later))


def finish_body(
    gathered,
    mean,
    table,
    depth,
    mask,
    kept,
    given,
    density_kept,
    density_given,
    out,
    loglik,
    density,
    stage,
    marks,
    classes,
    bins,
    total_pix,
):
    _, shells, width = kept.shape
    chip, core = position_of()
    pieces, copies = [], []
    for d in range(4):
        for k, (side, away, half) in enumerate(
            ((kept, density_kept, core), (given, density_given, 1 - core))
        ):
            pieces.append((side, d, offset_of(half, d, chip, width)))
            slot = 2 * d + k
            copies.append(pltpu.make_async_copy(away.at[d], density.at[slot], marks.at[slot]))
            copies[-1].start()
    row = jnp.broadcast_to(jnp.sum(gathered[...], axis=0), (8, 128))
    weighted = row[:1, :bins]
    total = pltpu.roll(row, 96, 1)[:1, :bins]
    norm = weighted / total_pix
    level = total / (total_pix * norm)
    drop = jnp.sum(table[...] * level, axis=1, keepdims=True)
    drop = jnp.broadcast_to(drop, (drop.shape[0], WIDE))
    for slot, (side, d, base) in enumerate(pieces):
        copies[slot].wait()
        for start in range(0, width, WIDE):
            here, away = slice(start, start + WIDE), pl.ds(base + start, WIDE)
            chosen = depth[:, away]
            less = drop[:shells]
            for c in range(1, classes):
                less = jnp.where(chosen == c, drop[c * shells : (c + 1) * shells], less)
            less = density[slot, :, here] * (mask[:, away] * less)
            stage[slot, :, here] = side[d, :, here] - less
        copies.append(
            pltpu.make_async_copy(
                stage.at[slot], out.at[:, pl.ds(base, width)], marks.at[8 + slot]
            )
        )
        copies[-1].start()
    average = mean[...]
    terms = total * jnp.log(average / norm) - average * (weighted / norm)
    lane = iota((1, 128), 1)
    logs = jnp.where(lane >= 64, row[:1], 0.0)
    value = jnp.sum(terms, axis=1, keepdims=True) + jnp.sum(logs, axis=1, keepdims=True)
    loglik[...] = value / (bins * total_pix)
    for copy in copies[8:]:
        copy.wait()


def finish(
    gathered, mean, table, depth, mask, kept, given, density_kept, density_given, total_pix
):
    _, shells, width = kept.shape
    pixels, bins = 8 * width, table.shape[1]
    classes = table.shape[0] // shells
    operands = in_vmem(gathered, mean, table, depth, mask, kept, given)
    return pl.pallas_call(
        functools.partial(finish_body, classes=classes, bins=bins, total_pix=total_pix),
        in_specs=[HERE] * 7 + [AWAY] * 2,
        out_specs=[AWAY, pl.BlockSpec()],
        out_shape=[
            jax.ShapeDtypeStruct((shells, pixels), jnp.float32),
            jax.ShapeDtypeStruct((1, 1), jnp.float32),
        ],
        scratch_shapes=[
            vmem(8, shells, width),
            vmem(8, shells, width),
            pltpu.SemaphoreType.DMA((16,)),
        ],
        compiler_params=LIMIT,
        name="finish",
    )(*operands, *in_hbm(density_kept, density_given))


def gradient_body(*refs, classes, bins, mine):
    quotients, refs = refs[:4], refs[4:]
    density_away, rest_away, depth, weights, partner, side = refs[:6]
    out, density, rest, marks = refs[6:]
    _, shells, width = out.shape
    sub = width // 2
    chip, core = position_of()
    half = core if mine else 1 - core
    loads = []
    for d in range(4):
        base = offset_of(half, d, chip, width)
        loads.append(
            (
                pltpu.make_async_copy(density_away.at[d], density.at[d], marks.at[d]),
                pltpu.make_async_copy(
                    rest_away.at[:, pl.ds(base, width)], rest.at[d], marks.at[4 + d]
                ),
            )
        )
        for load in loads[-1]:
            load.start()
    row = iota((shells, WIDE), 0)
    beside_partner = (row == 0) & (core == 1) | (row == shells - 1) & (core == 0)
    outside = (row == 0) & (core == 0) | (row == shells - 1) & (core == 1)
    filler = jnp.zeros((weights.shape[1] // 3 - 2 * bins, WIDE), jnp.float32)
    for d in range(4):
        base = offset_of(half, d, chip, width)
        for load in loads[d]:
            load.wait()
        for start in range(0, sub, WIDE):
            values = quotients[d][:, start : start + WIDE]
            high, low = split(jnp.concatenate([values, filler], axis=0))
            every = jnp.dot(
                weights[...],
                jnp.concatenate([high, low, high], axis=0),
                preferred_element_type=jnp.float32,
            )
            for k in range(2):
                here = slice(start + k * sub, start + k * sub + WIDE)
                away = pl.ds(base + (start + k * sub), WIDE)
                chosen = depth[:, away]
                begin = k * classes * shells
                back = every[begin : begin + shells]
                for c in range(1, classes):
                    begin += shells
                    back = jnp.where(chosen == c, every[begin : begin + shells], back)
                near = jnp.where(beside_partner, partner[:, away], 0.0)
                near = jnp.where(outside, side[:, away], near)
                out[d, :, here] = density[d, :, here] * back + (rest[d, :, here] + RADIAL * near)


def gradient(quotients, density, rest, depth, weights, partner, side, classes, bins, mine):
    shells, pixels = rest.shape
    width = pixels // 8
    operands = in_vmem(*quotients) + in_hbm(density, rest)
    operands += in_vmem(depth, weights, partner, side)
    return pl.pallas_call(
        functools.partial(gradient_body, classes=classes, bins=bins, mine=mine),
        in_specs=[HERE] * 4 + [AWAY] * 2 + [HERE] * 4,
        out_specs=HERE,
        out_shape=vmem(4, shells, width),
        scratch_shapes=[
            vmem(4, shells, width),
            vmem(4, shells, width),
            pltpu.SemaphoreType.DMA((8,)),
        ],
        compiler_params=LIMIT,
        name="gradient_kept" if mine else "gradient_given",
    )(*operands)


def pair_body(mine, partner, out):
    row = mine[...] + partner[...]
    out[...] = jnp.broadcast_to(row[None], out.shape)


def pair(mine, partner):
    return pl.pallas_call(
        pair_body,
        in_specs=[HERE] * 2,
        out_specs=HERE,
        out_shape=vmem(lax.axis_size("pix") * lax.axis_size("x"), 1, 128),
        compiler_params=LIMIT,
        name="pair",
    )(*in_vmem(mine, partner))


def swap(values):
    return lax.ppermute(values, "core", [(0, 1), (1, 0)])


def beside(values):
    count = lax.axis_size("x") * lax.axis_size("core")
    pairs = [(i, i + 1) for i in range(1, count - 1, 2)]
    return lax.ppermute(values, ("x", "core"), pairs + [(b, a) for a, b in pairs])


def along(values, step):
    count = lax.axis_size("x")
    return lax.ppermute(values, "x", [(i, (i + step) % count) for i in range(count)])


def across(values, start):
    pairs = [(i, i + 1) for i in range(start, lax.axis_size("pix") - 1, 2)]
    return lax.ppermute(values, "pix", pairs + [(b, a) for a, b in pairs])


def shards(field, momentum, kernels, depth_class, counts, mask, mean_counts, shell_scale):
    shells, pixels = field.shape
    classes, bins, _ = kernels.shape
    total_pix = pixels * lax.axis_size("pix")
    table = jnp.transpose(kernels, (0, 2, 1)).reshape(classes * shells, bins)

    given = project_given(
        field,
        momentum,
        depth_class.reshape(1, pixels),
        mask.reshape(1, pixels),
        table,
        classes,
        bins,
    )
    proj, density_given, place_given, field_kept, momentum_kept, depth, cover, weights = given
    proj_partner = swap(proj)
    proj_kept, density_kept, place_kept = project_kept(
        field_kept, momentum_kept, depth, weights, classes, bins
    )
    own, first, second, third, near, beyond = combine(
        proj_kept, proj_partner, place_given, place_kept
    )
    second = along(second, 2)
    first = along(first, 1)
    third = along(third, 3)
    near = across(near, 0)
    beyond = across(beyond, 1)
    own_counts, weights, square, mean, table, to_partner, to_side = prepare(
        counts,
        place_given,
        place_kept,
        own,
        table,
        shell_scale.reshape(1, shells),
        mean_counts.reshape(1, bins),
    )
    partner_row = swap(to_partner)
    side_row = beside(to_side)
    rest = stencil(place_given, place_kept, near, beyond, square)
    quotient, stats = ratio(own, first, second, third, own_counts, cover, rest)
    from_far = along(quotient, 2)
    from_back = along(quotient, 1)
    from_front = along(quotient, 3)
    partner_stats = swap(stats)
    stats = pair(stats, partner_stats)
    gathered = lax.all_to_all(stats, ("pix", "x"), 0, 0)
    mine = [quotient, from_front, from_far, from_back]
    theirs = [swap(q) for q in mine]

    common = (rest, depth, weights, partner_row, side_row, classes, bins)
    kept = gradient(mine, density_kept, *common, True)
    given = gradient(theirs, density_given, *common, False)
    out, loglik = finish(
        gathered, mean, table, depth, cover, kept, given, density_kept, density_given, total_pix
    )
    return out, loglik.reshape(())


def solution(mesh):
    grid = mesh.devices.reshape(mesh.devices.shape[0], -1, 2)
    split_mesh = Mesh(grid, ("pix", "x", "core"))
    shell = ("x", "core")
    placed = (
        P(shell, "pix"),
        P(shell, "pix"),
        P(None, None, shell),
        P("pix"),
        P(None, "pix"),
        P("pix"),
        P(),
        P(shell),
    )
    return jax.shard_map(
        shards,
        mesh=split_mesh,
        in_specs=placed,
        out_specs=(P(shell, "pix"), P()),
        check_vma=False,
    )
```

```python
import functools

import jax
import jax.numpy as jnp
from jax import lax
from jax.experimental import pallas as pl
from jax.experimental.pallas import tpu as pltpu
from jax.sharding import Mesh, PartitionSpec as P


CYCLE = 2048
LEAP = 0.1
ANGULAR = 0.5
RADIAL = 0.5
WIDE = 256


def split(values):
    high = values.astype(jnp.bfloat16)
    low = (values - high.astype(jnp.float32)).astype(jnp.bfloat16)
    return high, low


def iota(shape, dim):
    return lax.broadcasted_iota(jnp.int32, shape, dim)


def dot_nt(a, b):
    return lax.dot_general(a, b, (((1,), (1,)), ((), ())), preferred_element_type=jnp.float32)


def forward_weights(table, classes, bins, shells):
    rows, cols = classes * 2 * bins, 6 * shells
    spread = (iota((rows, bins), 0) % bins == iota((rows, bins), 1)).astype(jnp.bfloat16)
    same_class = iota((rows, classes * shells), 0) // (2 * bins) == (
        iota((rows, classes * shells), 1) // shells
    )
    place = (iota((classes * shells, cols), 0) % shells == iota((classes * shells, cols), 1) % shells)
    place = place.astype(jnp.bfloat16)
    parts = []
    for part in split(table):
        wide = jnp.where(same_class, dot_nt(spread, part), 0.0).astype(jnp.bfloat16)
        parts.append(jnp.dot(wide, place, preferred_element_type=jnp.float32))
    row, col = iota((rows, cols), 0), iota((rows, cols), 1)
    picked = jnp.where(col // (2 * shells) == 2, parts[1], parts[0])
    same_sub = (row // bins) % 2 == (col // shells) % 2
    return jnp.where(same_sub, picked, 0.0).astype(jnp.bfloat16)


def backward_weights(table, classes, bins, shells, depth):
    half = classes * shells
    rows, cols = 2 * half, 3 * depth
    place = iota((bins, cols), 0) == (iota((bins, cols), 1) % depth) % bins
    place = place.astype(jnp.bfloat16)
    parts = []
    for part in split(table):
        once = jnp.dot(part, place, preferred_element_type=jnp.float32)
        parts.append(jnp.concatenate([once, once], axis=0))
    row, col = iota((rows, cols), 0), iota((rows, cols), 1)
    picked = jnp.where(col // depth == 2, parts[1], parts[0])
    same_sub = row // half == (col % depth) // bins
    return jnp.where(same_sub, picked, 0.0).astype(jnp.bfloat16)


def packed_row(row, start, width, bins):
    first = row[:, pl.ds(start, WIDE)]
    second = row[:, pl.ds(start + width, WIDE)]
    return jnp.where(iota((2 * bins, WIDE), 0) < bins, first, second)


def position_of():
    return lax.axis_index("x"), lax.axis_index("core")


def offset_of(half, turn, chip, width):
    return pl.multiple_of((half * 4 + (chip + turn) % 4) * width, width)


def project_piece(
    d, base, field, momentum, depth, weights, proj, density, position, classes, bins
):
    sub = field.shape[2] // 2
    for start in range(0, sub, WIDE):
        halves = []
        for begin in (start, start + sub):
            here = slice(begin, begin + WIDE)
            place = field[d, :, here] + LEAP * momentum[d, :, here]
            values = jnp.exp(place)
            position[d, :, here] = place
            density[d, :, here] = values
            halves.append(values)
        high, low = split(jnp.concatenate(halves, axis=0))
        every = jnp.dot(
            weights[...],
            jnp.concatenate([high, low, high], axis=0),
            preferred_element_type=jnp.float32,
        )
        chosen = packed_row(depth, base + start, sub, bins)
        picked = every[: 2 * bins]
        for k in range(1, classes):
            picked = jnp.where(chosen == k, every[2 * bins * k : 2 * bins * (k + 1)], picked)
        proj[:, start : start + WIDE] = picked


FAR, REST = 2, (0, 1, 3)


def load_body(
    field,
    momentum,
    depth,
    mask,
    table_away,
    proj,
    density,
    position,
    field_given,
    momentum_given,
    field_kept,
    momentum_kept,
    depth_here,
    mask_here,
    weights,
    stage,
    table,
    marks,
    classes,
    bins,
):
    _, shells, width = field_given.shape
    chip, core = position_of()
    small = [
        pltpu.make_async_copy(table_away, table, marks.at[18]),
        pltpu.make_async_copy(depth, depth_here, marks.at[16]),
        pltpu.make_async_copy(mask, mask_here, marks.at[17]),
    ]

    def fetch(half, d, source, target, mark):
        begin = offset_of(half, d, chip, width)
        return pltpu.make_async_copy(
            source.at[:, pl.ds(begin, width)], target.at[d], marks.at[mark]
        )

    first, later = [], []
    for d in (FAR, *REST):
        group = first if d == FAR else later
        group.append(fetch(1 - core, d, field, field_given, 2 * d))
        group.append(fetch(1 - core, d, momentum, momentum_given, 2 * d + 1))
    for d in (FAR, *REST):
        later.append(fetch(core, d, field, field_kept, 8 + 2 * d))
        later.append(fetch(core, d, momentum, momentum_kept, 9 + 2 * d))
    for copy in small[:2] + first + later + small[2:]:
        copy.start()
    small[0].wait()
    weights[...] = forward_weights(table[...], classes, bins, shells)
    small[1].wait()
    for copy in first:
        copy.wait()
    project_piece(
        FAR,
        offset_of(1 - core, FAR, chip, width),
        field_given,
        momentum_given,
        depth_here,
        weights,
        proj,
        stage,
        position,
        classes,
        bins,
    )
    out = pltpu.make_async_copy(stage.at[FAR], density.at[FAR], marks.at[19])
    out.start()
    for copy in later + small[2:] + [out]:
        copy.wait()


def in_hbm(*values):
    return [pltpu.with_memory_space_constraint(v, pltpu.HBM) for v in values]


def in_vmem(*values):
    return [pltpu.with_memory_space_constraint(v, pltpu.VMEM) for v in values]


HERE = pl.BlockSpec(memory_space=pltpu.VMEM)
AWAY = pl.BlockSpec(memory_space=pltpu.HBM)


LIMIT = pltpu.CompilerParams(vmem_limit_bytes=16 << 20)


def vmem(*shape, dtype=jnp.float32):
    return pltpu.VMEM(shape, dtype)


def load(field, momentum, depth, mask, table, classes, bins):
    shells, pixels = field.shape
    width = pixels // 8
    outs = [
        vmem(2 * bins, width // 2),
        pltpu.HBM((4, shells, width), jnp.float32),
        vmem(4, shells, width),
        vmem(4, shells, width),
        vmem(4, shells, width),
        vmem(4, shells, width),
        vmem(4, shells, width),
        vmem(1, pixels, dtype=jnp.int32),
        vmem(1, pixels),
        vmem(classes * 2 * bins, 6 * shells, dtype=jnp.bfloat16),
    ]
    return pl.pallas_call(
        functools.partial(load_body, classes=classes, bins=bins),
        in_specs=[AWAY] * 5,
        out_specs=[HERE, AWAY] + [HERE] * (len(outs) - 2),
        out_shape=outs,
        scratch_shapes=[
            vmem(4, shells, width),
            vmem(*table.shape),
            pltpu.SemaphoreType.DMA((20,)),
        ],
        compiler_params=LIMIT,
        name="load",
    )(*in_hbm(field, momentum, depth, mask, table))


def project_rest_body(
    field,
    momentum,
    depth,
    weights,
    density_before,
    position_before,
    proj,
    density,
    position,
    stage,
    marks,
    mine,
    classes,
    bins,
):
    width = field.shape[2]
    chip, core = position_of()
    half = core if mine else 1 - core
    copies = []
    for k, d in enumerate(REST):
        project_piece(
            d,
            offset_of(half, d, chip, width),
            field,
            momentum,
            depth,
            weights,
            proj.at[k],
            stage,
            position,
            classes,
            bins,
        )
        copies.append(pltpu.make_async_copy(stage.at[d], density.at[d], marks.at[k]))
        copies[-1].start()
    for copy in copies:
        copy.wait()


def project_rest(field, momentum, depth, weights, density, position, mine, classes, bins):
    _, shells, width = field.shape
    return pl.pallas_call(
        functools.partial(project_rest_body, mine=mine, classes=classes, bins=bins),
        in_specs=[HERE] * 4 + [AWAY, HERE],
        out_specs=[HERE, AWAY, HERE],
        out_shape=[
            vmem(len(REST), 2 * bins, width // 2),
            pltpu.HBM((4, shells, width), jnp.float32),
            vmem(4, shells, width),
        ],
        scratch_shapes=[vmem(4, shells, width), pltpu.SemaphoreType.DMA((len(REST),))],
        input_output_aliases={4: 1, 5: 2},
        compiler_params=LIMIT,
        name="rest_kept" if mine else "rest_given",
    )(*in_vmem(field, momentum, depth, weights), *in_hbm(density), *in_vmem(position))


def project_far_body(
    field,
    momentum,
    depth,
    weights,
    partner,
    total,
    density,
    position,
    stage,
    proj,
    mark,
    classes,
    bins,
):
    width = field.shape[2]
    chip, core = position_of()
    project_piece(
        FAR,
        offset_of(core, FAR, chip, width),
        field,
        momentum,
        depth,
        weights,
        proj,
        stage,
        position,
        classes,
        bins,
    )
    copy = pltpu.make_async_copy(stage.at[FAR], density.at[FAR], mark)
    copy.start()
    total[...] = proj[...] + partner[...]
    copy.wait()


def project_far(field, momentum, depth, weights, partner, classes, bins):
    _, shells, width = field.shape
    return pl.pallas_call(
        functools.partial(project_far_body, classes=classes, bins=bins),
        in_specs=[HERE] * 5,
        out_specs=[HERE, AWAY, HERE],
        out_shape=[
            vmem(*partner.shape),
            pltpu.HBM((4, shells, width), jnp.float32),
            vmem(4, shells, width),
        ],
        scratch_shapes=[
            vmem(4, shells, width),
            vmem(*partner.shape),
            pltpu.SemaphoreType.DMA,
        ],
        compiler_params=LIMIT,
        name="far_kept",
    )(*in_vmem(field, momentum, depth, weights, partner))


def combine_body(kept, partner, given_place, kept_place, own, first, third, near, beyond):
    chip, core = position_of()
    for d, out in enumerate((own, first, third)):
        out[...] = kept[d] + partner[d]
    front, back = (4 - chip) % 4, (7 - chip) % 4
    edge = given_place.shape[2] - CYCLE
    even = lax.axis_index("pix") % 2 == 0

    def ends(low, high):
        head, tail = low[front, :, :CYCLE], high[back, :, edge:]
        near[...] = jnp.where(even, tail, head)
        beyond[...] = jnp.where(even, head, tail)

    pl.when(core == 0)(lambda: ends(kept_place, given_place))
    pl.when(core == 1)(lambda: ends(given_place, kept_place))


def combine(kept, partner, given_place, kept_place):
    _, rows, sub = kept.shape
    shells = given_place.shape[1]
    outs = [vmem(rows, sub)] * 3 + [vmem(shells, CYCLE)] * 2
    return pl.pallas_call(
        combine_body,
        in_specs=[HERE] * 4,
        out_specs=[HERE] * 5,
        out_shape=outs,
        compiler_params=LIMIT,
        name="combine",
    )(*in_vmem(kept, partner, given_place, kept_place))


def column(row, count):
    width = row.shape[1]
    at = iota((count, width), 0) % width == iota((count, width), 1)
    wide = jnp.broadcast_to(row, (8, width))
    return exact_rows(wide, at.astype(jnp.bfloat16))[:, :1]


def prepare_body(
    counts,
    given,
    kept,
    after,
    table,
    scale,
    mean,
    own,
    weights,
    square,
    means,
    kernels,
    to_partner,
    to_side,
    here,
    mark,
    deep,
):
    bins, part = here.shape
    shells = square.shape[0]
    chip, core = position_of()
    base = offset_of(core, 0, chip, part)
    copy = pltpu.make_async_copy(counts.at[:, pl.ds(base, part)], here, mark)
    copy.start()
    weights[...] = backward_weights(table[...], table.shape[0] // shells, bins, shells, deep)
    size = column(scale[...], shells)
    square[...] = jnp.broadcast_to(1.0 / (size * size), square.shape)
    means[...] = mean[...]
    kernels[...] = table[...]
    for d in range(4):
        for source, half in ((given, 1 - core), (kept, core)):
            begin = offset_of(half, d, chip, part)
            for start in range(0, part, 1024):
                first = source[d, :1, start : start + 1024]
                last = source[d, shells - 1 :, start : start + 1024]
                there = pl.ds(begin + start, 1024)
                to_partner[:, there] = jnp.where(core == 0, last, first)
                to_side[:, there] = jnp.where(core == 0, first, last)
    copy.wait()
    sub = part // 2
    for start in range(0, sub, 512):
        there = slice(start, start + 512)
        own[:bins, there] = here[:, there].astype(jnp.float32)
        own[bins:, there] = here[:, start + sub : start + sub + 512].astype(jnp.float32)


def prepare(counts, given, kept, after, table, scale, mean):
    bins, pixels = counts.shape
    shells = scale.shape[1]
    deep = -(-2 * bins // 16) * 16
    return pl.pallas_call(
        functools.partial(prepare_body, deep=deep),
        in_specs=[AWAY, HERE, HERE, HERE, pl.BlockSpec(), pl.BlockSpec(), pl.BlockSpec()],
        out_specs=[HERE] * 7,
        out_shape=[
            vmem(2 * bins, pixels // 16),
            vmem(2 * table.shape[0], 3 * deep, dtype=jnp.bfloat16),
            vmem(shells, 128),
            vmem(1, bins),
            vmem(*table.shape),
            vmem(1, pixels),
            vmem(1, pixels),
        ],
        scratch_shapes=[vmem(bins, pixels // 8, dtype=jnp.int32), pltpu.SemaphoreType.DMA],
        compiler_params=LIMIT,
        name="prepare",
    )(*in_hbm(counts), *in_vmem(given, kept, after), table, scale, mean)


def stencil_body(
    given, kept, near, beyond, scale, away, position, out, marks
):
    _, shells, width = given.shape
    pixels = 8 * width
    chip, core = position_of()
    even = lax.axis_index("pix") % 2 == 0
    position[:, :CYCLE] = jnp.where(even, beyond[...], near[...])
    position[:, CYCLE + pixels :] = jnp.where(even, near[...], beyond[...])
    for d in range(4):
        for source, half in ((given, 1 - core), (kept, core)):
            base = offset_of(half, d, chip, width)
            for start in range(0, width, 1024):
                values = source[d, :, start : start + 1024]
                position[:, pl.ds(CYCLE + base + start, 1024)] = values
    inverse = jnp.concatenate([scale[...]] * 4, axis=1)
    row = iota((shells, 512), 0)

    def step(i, carry):
        start = pl.multiple_of(i * 512, 512)
        near = position[:, pl.ds(CYCLE + start - 128, 512 + 256)]
        middle = near[:, 128:640]
        left = pltpu.roll(near, 1, 1)[:, 128:640]
        right = pltpu.roll(near, 767, 1)[:, 128:640]
        early = position[:, pl.ds(start, 512)]
        late = position[:, pl.ds(2 * CYCLE + start, 512)]
        angular = 4.0 * middle - left - right - early - late
        up = jnp.where(row == 0, 0.0, pltpu.roll(middle, 1, 0))
        down = jnp.where(row == shells - 1, 0.0, pltpu.roll(middle, shells - 1, 0))
        radial = 2.0 * middle - up - down
        out[:, pl.ds(start, 512)] = -middle * inverse - ANGULAR * angular - RADIAL * radial
        return carry

    copies = []
    steps = pixels // 4096
    for i in range(8):
        lax.fori_loop(i * steps, (i + 1) * steps, step, 0, unroll=4)
        piece = pl.ds(i * steps * 512, steps * 512)
        copies.append(pltpu.make_async_copy(out.at[:, piece], away.at[:, piece], marks.at[i]))
        copies[-1].start()
    for copy in copies:
        copy.wait()


def stencil(given, kept, before, after, scale):
    _, shells, width = given.shape
    pixels = 8 * width
    return pl.pallas_call(
        stencil_body,
        in_specs=[HERE] * 5,
        out_specs=AWAY,
        out_shape=pltpu.HBM((shells, pixels), jnp.float32),
        scratch_shapes=[
            vmem(shells, pixels + 2 * CYCLE),
            vmem(shells, pixels),
            pltpu.SemaphoreType.DMA((8,)),
        ],
        compiler_params=LIMIT,
        name="stencil",
    )(*in_vmem(given, kept, before, after, scale))


def exact_rows(values, ones):
    total = 0.0
    for _ in range(3):
        part = values.astype(jnp.bfloat16)
        values = values - part.astype(jnp.float32)
        total = total + dot_nt(ones, part)
    return total


def ratio_body(own, first, second, third, counts, mask, later, out, stats):
    rows, sub = out.shape
    bins = rows // 2
    chip, core = position_of()
    base = offset_of(core, 0, chip, 2 * sub)
    weighted = logs = totals = jnp.zeros((rows, 128), jnp.float32)
    for start in range(0, sub, WIDE):
        here = slice(start, start + WIDE)
        proj = own[:, here] + first[:, here] + second[:, here] + third[:, here]
        some = counts[:, here]
        out[:, here] = some / proj
        covered = proj * packed_row(mask, base + start, sub, bins)
        term = some * jnp.log(covered)
        for lane in range(0, WIDE, 128):
            weighted = weighted + covered[:, lane : lane + 128]
            logs = logs + term[:, lane : lane + 128]
            totals = totals + some[:, lane : lane + 128]
    gap = jnp.zeros((32 - bins, 128), jnp.float32)
    sums = jnp.concatenate(
        [
            weighted[:bins] + weighted[bins:],
            gap,
            totals[:bins] + totals[bins:],
            gap,
            logs,
            jnp.zeros((64 - rows, 128), jnp.float32),
        ],
        axis=0,
    )
    row = exact_rows(sums, jnp.ones((8, 128), jnp.bfloat16))[:1]
    stats[...] = jnp.broadcast_to(row.reshape((1,) * (stats.ndim - 1) + (128,)), stats.shape)


def ratio(own, first, second, third, counts, mask, later):
    return pl.pallas_call(
        ratio_body,
        in_specs=[HERE] * 6 + [AWAY],
        out_specs=[HERE, HERE],
        out_shape=[
            vmem(*own.shape),
            vmem(1, 128),
        ],
        compiler_params=LIMIT,
        name="ratio",
    )(*in_vmem(own, first, second, third, counts, mask), *in_hbm(later))


def finish_body(
    gathered,
    mean,
    table,
    depth,
    mask,
    kept,
    given,
    density_kept,
    density_given,
    out,
    loglik,
    density,
    stage,
    marks,
    classes,
    bins,
    total_pix,
):
    _, shells, width = kept.shape
    chip, core = position_of()
    pieces, copies = [], []
    for d in range(4):
        for k, (side, away, half) in enumerate(
            ((kept, density_kept, core), (given, density_given, 1 - core))
        ):
            pieces.append((side, d, offset_of(half, d, chip, width)))
            slot = 2 * d + k
            copies.append(pltpu.make_async_copy(away.at[d], density.at[slot], marks.at[slot]))
            copies[-1].start()
    row = jnp.broadcast_to(jnp.sum(gathered[...], axis=0), (8, 128))
    weighted = row[:1, :bins]
    total = pltpu.roll(row, 96, 1)[:1, :bins]
    norm = weighted / total_pix
    level = total / (total_pix * norm)
    drop = jnp.sum(table[...] * level, axis=1, keepdims=True)
    drop = jnp.broadcast_to(drop, (drop.shape[0], WIDE))
    for slot, (side, d, base) in enumerate(pieces):
        copies[slot].wait()
        for start in range(0, width, WIDE):
            here, away = slice(start, start + WIDE), pl.ds(base + start, WIDE)
            chosen = depth[:, away]
            less = drop[:shells]
            for c in range(1, classes):
                less = jnp.where(chosen == c, drop[c * shells : (c + 1) * shells], less)
            less = density[slot, :, here] * (mask[:, away] * less)
            stage[slot, :, here] = side[d, :, here] - less
        copies.append(
            pltpu.make_async_copy(
                stage.at[slot], out.at[:, pl.ds(base, width)], marks.at[8 + slot]
            )
        )
        copies[-1].start()
    average = mean[...]
    terms = total * jnp.log(average / norm) - average * (weighted / norm)
    lane = iota((1, 128), 1)
    logs = jnp.where(lane >= 64, row[:1], 0.0)
    value = jnp.sum(terms, axis=1, keepdims=True) + jnp.sum(logs, axis=1, keepdims=True)
    loglik[...] = value / (bins * total_pix)
    for copy in copies[8:]:
        copy.wait()


def finish(
    gathered, mean, table, depth, mask, kept, given, density_kept, density_given, total_pix
):
    _, shells, width = kept.shape
    pixels, bins = 8 * width, table.shape[1]
    classes = table.shape[0] // shells
    operands = in_vmem(gathered, mean, table, depth, mask, kept, given)
    return pl.pallas_call(
        functools.partial(finish_body, classes=classes, bins=bins, total_pix=total_pix),
        in_specs=[HERE] * 7 + [AWAY] * 2,
        out_specs=[AWAY, pl.BlockSpec()],
        out_shape=[
            jax.ShapeDtypeStruct((shells, pixels), jnp.float32),
            jax.ShapeDtypeStruct((1, 1), jnp.float32),
        ],
        scratch_shapes=[
            vmem(8, shells, width),
            vmem(8, shells, width),
            pltpu.SemaphoreType.DMA((16,)),
        ],
        compiler_params=LIMIT,
        name="finish",
    )(*operands, *in_hbm(density_kept, density_given))


def gradient_body(*refs, classes, bins, mine):
    quotients, refs = refs[:4], refs[4:]
    if mine:
        density_away, rest_away, density_next, depth, weights, partner, side = refs[:7]
        out, density_there, rest_there, density, rest, marks = refs[7:]
    else:
        density, rest, depth, weights, partner, side, out = refs
    _, shells, width = out.shape
    sub = width // 2
    chip, core = position_of()
    half = core if mine else 1 - core
    loads = [()] * 4
    later = []
    if mine:

        def fetch(half, d, source, target, mark):
            base = offset_of(half, d, chip, width)
            return pltpu.make_async_copy(
                source.at[:, pl.ds(base, width)], target.at[d], marks.at[mark]
            )

        for d in range(4):
            loads[d] = (
                pltpu.make_async_copy(density_away.at[d], density.at[d], marks.at[d]),
                fetch(half, d, rest_away, rest, 4 + d),
            )
            later.append(
                pltpu.make_async_copy(density_next.at[d], density_there.at[d], marks.at[8 + d])
            )
            later.append(fetch(1 - half, d, rest_away, rest_there, 12 + d))
        for load in [load for pair in loads for load in pair] + later:
            load.start()
    row = iota((shells, WIDE), 0)
    beside_partner = (row == 0) & (core == 1) | (row == shells - 1) & (core == 0)
    outside = (row == 0) & (core == 0) | (row == shells - 1) & (core == 1)
    filler = jnp.zeros((weights.shape[1] // 3 - 2 * bins, WIDE), jnp.float32)
    for d in range(4):
        base = offset_of(half, d, chip, width)
        for load in loads[d]:
            load.wait()
        for start in range(0, sub, WIDE):
            values = quotients[d][:, start : start + WIDE]
            high, low = split(jnp.concatenate([values, filler], axis=0))
            every = jnp.dot(
                weights[...],
                jnp.concatenate([high, low, high], axis=0),
                preferred_element_type=jnp.float32,
            )
            for k in range(2):
                here = slice(start + k * sub, start + k * sub + WIDE)
                away = pl.ds(base + (start + k * sub), WIDE)
                chosen = depth[:, away]
                begin = k * classes * shells
                back = every[begin : begin + shells]
                for c in range(1, classes):
                    begin += shells
                    back = jnp.where(chosen == c, every[begin : begin + shells], back)
                near = jnp.where(beside_partner, partner[:, away], 0.0)
                near = jnp.where(outside, side[:, away], near)
                out[d, :, here] = density[d, :, here] * back + (rest[d, :, here] + RADIAL * near)
    for load in later:
        load.wait()


def gradient_kept(quotients, density, rest, next_density, common, classes, bins):
    _, shells, width = density.shape
    return pl.pallas_call(
        functools.partial(gradient_body, classes=classes, bins=bins, mine=True),
        in_specs=[HERE] * 4 + [AWAY] * 3 + [HERE] * 4,
        out_specs=[HERE] * 3,
        out_shape=[vmem(4, shells, width)] * 3,
        scratch_shapes=[
            vmem(4, shells, width),
            vmem(4, shells, width),
            pltpu.SemaphoreType.DMA((16,)),
        ],
        compiler_params=LIMIT,
        name="gradient_kept",
    )(*in_vmem(*quotients), *in_hbm(density, rest, next_density), *in_vmem(*common))


def gradient_given(quotients, density, rest, common, classes, bins):
    return pl.pallas_call(
        functools.partial(gradient_body, classes=classes, bins=bins, mine=False),
        in_specs=[HERE] * 10,
        out_specs=HERE,
        out_shape=vmem(*density.shape),
        compiler_params=LIMIT,
        name="gradient_given",
    )(*in_vmem(*quotients, density, rest, *common))


def pair_body(mine, partner, out):
    row = mine[...] + partner[...]
    out[...] = jnp.broadcast_to(row[None], out.shape)


def pair(mine, partner):
    return pl.pallas_call(
        pair_body,
        in_specs=[HERE] * 2,
        out_specs=HERE,
        out_shape=vmem(lax.axis_size("pix") * lax.axis_size("x"), 1, 128),
        compiler_params=LIMIT,
        name="pair",
    )(*in_vmem(mine, partner))


def swap(values):
    return lax.ppermute(values, "core", [(0, 1), (1, 0)])


def beside(values):
    count = lax.axis_size("x") * lax.axis_size("core")
    pairs = [(i, i + 1) for i in range(1, count - 1, 2)]
    return lax.ppermute(values, ("x", "core"), pairs + [(b, a) for a, b in pairs])


def along(values, step):
    count = lax.axis_size("x")
    return lax.ppermute(values, "x", [(i, (i + step) % count) for i in range(count)])


def across(values, start):
    pairs = [(i, i + 1) for i in range(start, lax.axis_size("pix") - 1, 2)]
    return lax.ppermute(values, "pix", pairs + [(b, a) for a, b in pairs])


def shards(field, momentum, kernels, depth_class, counts, mask, mean_counts, shell_scale):
    shells, pixels = field.shape
    classes, bins, _ = kernels.shape
    total_pix = pixels * lax.axis_size("pix")
    table = jnp.transpose(kernels, (0, 2, 1)).reshape(classes * shells, bins)

    loaded = load(
        field,
        momentum,
        depth_class.reshape(1, pixels),
        mask.reshape(1, pixels),
        table,
        classes,
        bins,
    )
    proj, density_given, place_given, field_given, momentum_given = loaded[:5]
    field_kept, momentum_kept, depth, cover, weights = loaded[5:]
    partner_far = swap(proj)
    proj, density_given, place_given = project_rest(
        field_given,
        momentum_given,
        depth,
        weights,
        density_given,
        place_given,
        False,
        classes,
        bins,
    )
    partner = swap(proj)
    second, density_kept, place_kept = project_far(
        field_kept, momentum_kept, depth, weights, partner_far, classes, bins
    )
    second = along(second, 2)
    proj, density_kept, place_kept = project_rest(
        field_kept, momentum_kept, depth, weights, density_kept, place_kept, True, classes, bins
    )
    own, first, third, near, beyond = combine(proj, partner, place_given, place_kept)
    first = along(first, 1)
    third = along(third, 3)
    near = across(near, 0)
    beyond = across(beyond, 1)
    own_counts, weights, square, mean, table, to_partner, to_side = prepare(
        counts,
        place_given,
        place_kept,
        own,
        table,
        shell_scale.reshape(1, shells),
        mean_counts.reshape(1, bins),
    )
    partner_row = swap(to_partner)
    side_row = beside(to_side)
    rest = stencil(place_given, place_kept, near, beyond, square)
    quotient, stats = ratio(own, first, second, third, own_counts, cover, rest)
    from_far = along(quotient, 2)
    from_back = along(quotient, 1)
    from_front = along(quotient, 3)
    partner_stats = swap(stats)
    stats = pair(stats, partner_stats)
    gathered = lax.all_to_all(stats, ("pix", "x"), 0, 0)
    mine = [quotient, from_front, from_far, from_back]
    theirs = [swap(q) for q in mine]

    common = (depth, weights, partner_row, side_row)
    kept, density_there, rest_there = gradient_kept(
        mine, density_kept, rest, density_given, common, classes, bins
    )
    given = gradient_given(theirs, density_there, rest_there, common, classes, bins)
    out, loglik = finish(
        gathered, mean, table, depth, cover, kept, given, density_kept, density_given, total_pix
    )
    return out, loglik.reshape(())


def solution(mesh):
    grid = mesh.devices.reshape(mesh.devices.shape[0], -1, 2)
    split_mesh = Mesh(grid, ("pix", "x", "core"))
    shell = ("x", "core")
    placed = (
        P(shell, "pix"),
        P(shell, "pix"),
        P(None, None, shell),
        P("pix"),
        P(None, "pix"),
        P("pix"),
        P(),
        P(shell),
    )
    return jax.shard_map(
        shards,
        mesh=split_mesh,
        in_specs=placed,
        out_specs=(P(shell, "pix"), P()),
        check_vma=False,
    )
```

```python
import functools

import jax
import jax.numpy as jnp
from jax import lax
from jax.experimental import pallas as pl
from jax.experimental.pallas import tpu as pltpu
from jax.sharding import Mesh, PartitionSpec as P


CYCLE = 2048
LEAP = 0.1
ANGULAR = 0.5
RADIAL = 0.5
WIDE = 256


def split(values):
    high = values.astype(jnp.bfloat16)
    low = (values - high.astype(jnp.float32)).astype(jnp.bfloat16)
    return high, low


def iota(shape, dim):
    return lax.broadcasted_iota(jnp.int32, shape, dim)


def dot_nt(a, b):
    return lax.dot_general(a, b, (((1,), (1,)), ((), ())), preferred_element_type=jnp.float32)


def forward_weights(table, classes, bins, shells):
    rows, cols = classes * 2 * bins, 6 * shells
    spread = (iota((rows, bins), 0) % bins == iota((rows, bins), 1)).astype(jnp.bfloat16)
    same_class = iota((rows, classes * shells), 0) // (2 * bins) == (
        iota((rows, classes * shells), 1) // shells
    )
    place = (iota((classes * shells, cols), 0) % shells == iota((classes * shells, cols), 1) % shells)
    place = place.astype(jnp.bfloat16)
    parts = []
    for part in split(table):
        wide = jnp.where(same_class, dot_nt(spread, part), 0.0).astype(jnp.bfloat16)
        parts.append(jnp.dot(wide, place, preferred_element_type=jnp.float32))
    row, col = iota((rows, cols), 0), iota((rows, cols), 1)
    picked = jnp.where(col // (2 * shells) == 2, parts[1], parts[0])
    same_sub = (row // bins) % 2 == (col // shells) % 2
    return jnp.where(same_sub, picked, 0.0).astype(jnp.bfloat16)


def backward_weights(table, classes, bins, shells, depth):
    half = classes * shells
    rows, cols = 2 * half, 3 * depth
    place = iota((bins, cols), 0) == (iota((bins, cols), 1) % depth) % bins
    place = place.astype(jnp.bfloat16)
    parts = []
    for part in split(table):
        once = jnp.dot(part, place, preferred_element_type=jnp.float32)
        parts.append(jnp.concatenate([once, once], axis=0))
    row, col = iota((rows, cols), 0), iota((rows, cols), 1)
    picked = jnp.where(col // depth == 2, parts[1], parts[0])
    same_sub = row // half == (col % depth) // bins
    return jnp.where(same_sub, picked, 0.0).astype(jnp.bfloat16)


def packed_row(row, start, width, bins):
    first = row[:, pl.ds(start, WIDE)]
    second = row[:, pl.ds(start + width, WIDE)]
    return jnp.where(iota((2 * bins, WIDE), 0) < bins, first, second)


def position_of():
    return lax.axis_index("x"), lax.axis_index("core")


def offset_of(half, turn, chip, width):
    return pl.multiple_of((half * 4 + (chip + turn) % 4) * width, width)


def project_piece(
    d, base, field, momentum, depth, weights, proj, density, position, classes, bins
):
    sub = field.shape[2] // 2
    for start in range(0, sub, WIDE):
        halves = []
        for begin in (start, start + sub):
            here = slice(begin, begin + WIDE)
            place = field[d, :, here] + LEAP * momentum[d, :, here]
            values = jnp.exp(place)
            position[d, :, here] = place
            density[d, :, here] = values
            halves.append(values)
        high, low = split(jnp.concatenate(halves, axis=0))
        every = jnp.dot(
            weights[...],
            jnp.concatenate([high, low, high], axis=0),
            preferred_element_type=jnp.float32,
        )
        chosen = packed_row(depth, base + start, sub, bins)
        picked = every[: 2 * bins]
        for k in range(1, classes):
            picked = jnp.where(chosen == k, every[2 * bins * k : 2 * bins * (k + 1)], picked)
        proj[:, start : start + WIDE] = picked


FAR, REST = 2, (0, 1, 3)


def load_body(
    field,
    momentum,
    depth,
    mask,
    table_away,
    proj,
    density,
    position,
    field_given,
    momentum_given,
    field_kept,
    momentum_kept,
    depth_here,
    mask_here,
    weights,
    stage,
    table,
    marks,
    classes,
    bins,
):
    _, shells, width = field_given.shape
    chip, core = position_of()
    small = [
        pltpu.make_async_copy(table_away, table, marks.at[18]),
        pltpu.make_async_copy(depth, depth_here, marks.at[16]),
        pltpu.make_async_copy(mask, mask_here, marks.at[17]),
    ]

    def fetch(half, d, source, target, mark):
        begin = offset_of(half, d, chip, width)
        return pltpu.make_async_copy(
            source.at[:, pl.ds(begin, width)], target.at[d], marks.at[mark]
        )

    first, later = [], []
    for d in (FAR, *REST):
        group = first if d == FAR else later
        group.append(fetch(1 - core, d, field, field_given, 2 * d))
        group.append(fetch(1 - core, d, momentum, momentum_given, 2 * d + 1))
    for d in (FAR, *REST):
        later.append(fetch(core, d, field, field_kept, 8 + 2 * d))
        later.append(fetch(core, d, momentum, momentum_kept, 9 + 2 * d))
    for copy in small[:2] + first + later + small[2:]:
        copy.start()
    small[0].wait()
    weights[...] = forward_weights(table[...], classes, bins, shells)
    small[1].wait()
    for copy in first:
        copy.wait()
    project_piece(
        FAR,
        offset_of(1 - core, FAR, chip, width),
        field_given,
        momentum_given,
        depth_here,
        weights,
        proj,
        stage,
        position,
        classes,
        bins,
    )
    out = pltpu.make_async_copy(stage.at[FAR], density.at[FAR], marks.at[19])
    out.start()
    for copy in later + small[2:] + [out]:
        copy.wait()


def in_hbm(*values):
    return [pltpu.with_memory_space_constraint(v, pltpu.HBM) for v in values]


def in_vmem(*values):
    return [pltpu.with_memory_space_constraint(v, pltpu.VMEM) for v in values]


HERE = pl.BlockSpec(memory_space=pltpu.VMEM)
AWAY = pl.BlockSpec(memory_space=pltpu.HBM)


LIMIT = pltpu.CompilerParams(vmem_limit_bytes=16 << 20)


def vmem(*shape, dtype=jnp.float32):
    return pltpu.VMEM(shape, dtype)


def load(field, momentum, depth, mask, table, classes, bins):
    shells, pixels = field.shape
    width = pixels // 8
    outs = [
        vmem(2 * bins, width // 2),
        pltpu.HBM((4, shells, width), jnp.float32),
        vmem(4, shells, width),
        vmem(4, shells, width),
        vmem(4, shells, width),
        vmem(4, shells, width),
        vmem(4, shells, width),
        vmem(1, pixels, dtype=jnp.int32),
        vmem(1, pixels),
        vmem(classes * 2 * bins, 6 * shells, dtype=jnp.bfloat16),
    ]
    return pl.pallas_call(
        functools.partial(load_body, classes=classes, bins=bins),
        in_specs=[AWAY] * 5,
        out_specs=[HERE, AWAY] + [HERE] * (len(outs) - 2),
        out_shape=outs,
        scratch_shapes=[
            vmem(4, shells, width),
            vmem(*table.shape),
            pltpu.SemaphoreType.DMA((20,)),
        ],
        compiler_params=LIMIT,
        name="load",
    )(*in_hbm(field, momentum, depth, mask, table))


def project_rest_body(
    field,
    momentum,
    depth,
    weights,
    density_before,
    position_before,
    proj,
    density,
    position,
    stage,
    marks,
    mine,
    classes,
    bins,
):
    width = field.shape[2]
    chip, core = position_of()
    half = core if mine else 1 - core
    copies = []
    if mine:
        copies.append(
            pltpu.make_async_copy(density_before.at[FAR], density.at[FAR], marks.at[len(REST)])
        )
        copies[-1].start()
    for k, d in enumerate(REST):
        project_piece(
            d,
            offset_of(half, d, chip, width),
            field,
            momentum,
            depth,
            weights,
            proj.at[k],
            stage,
            position,
            classes,
            bins,
        )
        copies.append(pltpu.make_async_copy(stage.at[d], density.at[d], marks.at[k]))
        copies[-1].start()
    for copy in copies:
        copy.wait()


def project_rest(field, momentum, depth, weights, density, position, mine, classes, bins):
    _, shells, width = field.shape
    return pl.pallas_call(
        functools.partial(project_rest_body, mine=mine, classes=classes, bins=bins),
        in_specs=[HERE] * 4 + [HERE if mine else AWAY, HERE],
        out_specs=[HERE, AWAY, HERE],
        out_shape=[
            vmem(len(REST), 2 * bins, width // 2),
            pltpu.HBM((4, shells, width), jnp.float32),
            vmem(4, shells, width),
        ],
        scratch_shapes=[vmem(4, shells, width), pltpu.SemaphoreType.DMA((4,))],
        input_output_aliases={5: 2} if mine else {4: 1, 5: 2},
        compiler_params=LIMIT,
        name="rest_kept" if mine else "rest_given",
    )(
        *in_vmem(field, momentum, depth, weights),
        *(in_vmem(density) if mine else in_hbm(density)),
        *in_vmem(position),
    )


def project_far_body(
    field,
    momentum,
    depth,
    weights,
    partner,
    total,
    stage,
    position,
    proj,
    classes,
    bins,
):
    width = field.shape[2]
    chip, core = position_of()
    project_piece(
        FAR,
        offset_of(core, FAR, chip, width),
        field,
        momentum,
        depth,
        weights,
        proj,
        stage,
        position,
        classes,
        bins,
    )
    total[...] = proj[...] + partner[...]


def project_far(field, momentum, depth, weights, partner, classes, bins):
    _, shells, width = field.shape
    return pl.pallas_call(
        functools.partial(project_far_body, classes=classes, bins=bins),
        in_specs=[HERE] * 5,
        out_specs=[HERE] * 3,
        out_shape=[
            vmem(*partner.shape),
            vmem(4, shells, width),
            vmem(4, shells, width),
        ],
        scratch_shapes=[vmem(*partner.shape)],
        compiler_params=LIMIT,
        name="far_kept",
    )(*in_vmem(field, momentum, depth, weights, partner))


def combine_body(kept, partner, given_place, kept_place, own, first, third, near, beyond):
    chip, core = position_of()
    for d, out in enumerate((own, first, third)):
        out[...] = kept[d] + partner[d]
    front, back = (4 - chip) % 4, (7 - chip) % 4
    edge = given_place.shape[2] - CYCLE
    even = lax.axis_index("pix") % 2 == 0

    def ends(low, high):
        head, tail = low[front, :, :CYCLE], high[back, :, edge:]
        near[...] = jnp.where(even, tail, head)
        beyond[...] = jnp.where(even, head, tail)

    pl.when(core == 0)(lambda: ends(kept_place, given_place))
    pl.when(core == 1)(lambda: ends(given_place, kept_place))


def combine(kept, partner, given_place, kept_place):
    _, rows, sub = kept.shape
    shells = given_place.shape[1]
    outs = [vmem(rows, sub)] * 3 + [vmem(shells, CYCLE)] * 2
    return pl.pallas_call(
        combine_body,
        in_specs=[HERE] * 4,
        out_specs=[HERE] * 5,
        out_shape=outs,
        compiler_params=LIMIT,
        name="combine",
    )(*in_vmem(kept, partner, given_place, kept_place))


def column(row, count):
    width = row.shape[1]
    at = iota((count, width), 0) % width == iota((count, width), 1)
    wide = jnp.broadcast_to(row, (8, width))
    return exact_rows(wide, at.astype(jnp.bfloat16))[:, :1]


def prepare_body(
    counts,
    given,
    kept,
    after,
    table,
    scale,
    mean,
    own,
    weights,
    square,
    means,
    kernels,
    to_partner,
    to_side,
    here,
    mark,
    deep,
):
    bins, part = here.shape
    shells = square.shape[0]
    chip, core = position_of()
    base = offset_of(core, 0, chip, part)
    copy = pltpu.make_async_copy(counts.at[:, pl.ds(base, part)], here, mark)
    copy.start()
    weights[...] = backward_weights(table[...], table.shape[0] // shells, bins, shells, deep)
    size = column(scale[...], shells)
    square[...] = jnp.broadcast_to(1.0 / (size * size), square.shape)
    means[...] = mean[...]
    kernels[...] = table[...]
    for d in range(4):
        for source, half in ((given, 1 - core), (kept, core)):
            begin = offset_of(half, d, chip, part)
            for start in range(0, part, 1024):
                first = source[d, :1, start : start + 1024]
                last = source[d, shells - 1 :, start : start + 1024]
                there = pl.ds(begin + start, 1024)
                to_partner[:, there] = jnp.where(core == 0, last, first)
                to_side[:, there] = jnp.where(core == 0, first, last)
    copy.wait()
    sub = part // 2
    for start in range(0, sub, 512):
        there = slice(start, start + 512)
        own[:bins, there] = here[:, there].astype(jnp.float32)
        own[bins:, there] = here[:, start + sub : start + sub + 512].astype(jnp.float32)


def prepare(counts, given, kept, after, table, scale, mean):
    bins, pixels = counts.shape
    shells = scale.shape[1]
    deep = -(-2 * bins // 16) * 16
    return pl.pallas_call(
        functools.partial(prepare_body, deep=deep),
        in_specs=[AWAY, HERE, HERE, HERE, pl.BlockSpec(), pl.BlockSpec(), pl.BlockSpec()],
        out_specs=[HERE] * 7,
        out_shape=[
            vmem(2 * bins, pixels // 16),
            vmem(2 * table.shape[0], 3 * deep, dtype=jnp.bfloat16),
            vmem(shells, 128),
            vmem(1, bins),
            vmem(*table.shape),
            vmem(1, pixels),
            vmem(1, pixels),
        ],
        scratch_shapes=[vmem(bins, pixels // 8, dtype=jnp.int32), pltpu.SemaphoreType.DMA],
        compiler_params=LIMIT,
        name="prepare",
    )(*in_hbm(counts), *in_vmem(given, kept, after), table, scale, mean)


def stencil_body(
    given, kept, near, beyond, scale, away, position, out, marks
):
    _, shells, width = given.shape
    pixels = 8 * width
    chip, core = position_of()
    even = lax.axis_index("pix") % 2 == 0
    position[:, :CYCLE] = jnp.where(even, beyond[...], near[...])
    position[:, CYCLE + pixels :] = jnp.where(even, near[...], beyond[...])
    for d in range(4):
        for source, half in ((given, 1 - core), (kept, core)):
            base = offset_of(half, d, chip, width)
            for start in range(0, width, 1024):
                values = source[d, :, start : start + 1024]
                position[:, pl.ds(CYCLE + base + start, 1024)] = values
    inverse = jnp.concatenate([scale[...]] * 4, axis=1)
    row = iota((shells, 512), 0)

    def step(i, carry):
        start = pl.multiple_of(i * 512, 512)
        near = position[:, pl.ds(CYCLE + start - 128, 512 + 256)]
        middle = near[:, 128:640]
        left = pltpu.roll(near, 1, 1)[:, 128:640]
        right = pltpu.roll(near, 767, 1)[:, 128:640]
        early = position[:, pl.ds(start, 512)]
        late = position[:, pl.ds(2 * CYCLE + start, 512)]
        angular = 4.0 * middle - left - right - early - late
        up = jnp.where(row == 0, 0.0, pltpu.roll(middle, 1, 0))
        down = jnp.where(row == shells - 1, 0.0, pltpu.roll(middle, shells - 1, 0))
        radial = 2.0 * middle - up - down
        out[:, pl.ds(start, 512)] = -middle * inverse - ANGULAR * angular - RADIAL * radial
        return carry

    copies = []
    steps = pixels // 4096
    for i in range(8):
        lax.fori_loop(i * steps, (i + 1) * steps, step, 0, unroll=4)
        piece = pl.ds(i * steps * 512, steps * 512)
        copies.append(pltpu.make_async_copy(out.at[:, piece], away.at[:, piece], marks.at[i]))
        copies[-1].start()
    for copy in copies:
        copy.wait()


def stencil(given, kept, before, after, scale):
    _, shells, width = given.shape
    pixels = 8 * width
    return pl.pallas_call(
        stencil_body,
        in_specs=[HERE] * 5,
        out_specs=AWAY,
        out_shape=pltpu.HBM((shells, pixels), jnp.float32),
        scratch_shapes=[
            vmem(shells, pixels + 2 * CYCLE),
            vmem(shells, pixels),
            pltpu.SemaphoreType.DMA((8,)),
        ],
        compiler_params=LIMIT,
        name="stencil",
    )(*in_vmem(given, kept, before, after, scale))


def exact_rows(values, ones):
    total = 0.0
    for _ in range(3):
        part = values.astype(jnp.bfloat16)
        values = values - part.astype(jnp.float32)
        total = total + dot_nt(ones, part)
    return total


def ratio_body(own, first, second, third, counts, mask, later, out, stats):
    rows, sub = out.shape
    bins = rows // 2
    chip, core = position_of()
    base = offset_of(core, 0, chip, 2 * sub)
    weighted = logs = totals = jnp.zeros((rows, 128), jnp.float32)
    for start in range(0, sub, WIDE):
        here = slice(start, start + WIDE)
        proj = own[:, here] + first[:, here] + second[:, here] + third[:, here]
        some = counts[:, here]
        out[:, here] = some / proj
        covered = proj * packed_row(mask, base + start, sub, bins)
        term = some * jnp.log(covered)
        for lane in range(0, WIDE, 128):
            weighted = weighted + covered[:, lane : lane + 128]
            logs = logs + term[:, lane : lane + 128]
            totals = totals + some[:, lane : lane + 128]
    gap = jnp.zeros((32 - bins, 128), jnp.float32)
    sums = jnp.concatenate(
        [
            weighted[:bins] + weighted[bins:],
            gap,
            totals[:bins] + totals[bins:],
            gap,
            logs,
            jnp.zeros((64 - rows, 128), jnp.float32),
        ],
        axis=0,
    )
    row = exact_rows(sums, jnp.ones((8, 128), jnp.bfloat16))[:1]
    stats[...] = jnp.broadcast_to(row.reshape((1,) * (stats.ndim - 1) + (128,)), stats.shape)


def ratio(own, first, second, third, counts, mask, later):
    return pl.pallas_call(
        ratio_body,
        in_specs=[HERE] * 6 + [AWAY],
        out_specs=[HERE, HERE],
        out_shape=[
            vmem(*own.shape),
            vmem(1, 128),
        ],
        compiler_params=LIMIT,
        name="ratio",
    )(*in_vmem(own, first, second, third, counts, mask), *in_hbm(later))


def finish_body(
    gathered,
    mean,
    table,
    depth,
    mask,
    kept,
    given,
    density_kept,
    density_given,
    out,
    loglik,
    density,
    stage,
    marks,
    classes,
    bins,
    total_pix,
):
    _, shells, width = kept.shape
    chip, core = position_of()
    pieces, copies = [], []
    for d in range(4):
        for k, (side, away, half) in enumerate(
            ((kept, density_kept, core), (given, density_given, 1 - core))
        ):
            pieces.append((side, d, offset_of(half, d, chip, width)))
            slot = 2 * d + k
            copies.append(pltpu.make_async_copy(away.at[d], density.at[slot], marks.at[slot]))
            copies[-1].start()
    row = jnp.broadcast_to(jnp.sum(gathered[...], axis=0), (8, 128))
    weighted = row[:1, :bins]
    total = pltpu.roll(row, 96, 1)[:1, :bins]
    norm = weighted / total_pix
    level = total / (total_pix * norm)
    drop = jnp.sum(table[...] * level, axis=1, keepdims=True)
    drop = jnp.broadcast_to(drop, (drop.shape[0], WIDE))
    for slot, (side, d, base) in enumerate(pieces):
        copies[slot].wait()
        for start in range(0, width, WIDE):
            here, away = slice(start, start + WIDE), pl.ds(base + start, WIDE)
            chosen = depth[:, away]
            less = drop[:shells]
            for c in range(1, classes):
                less = jnp.where(chosen == c, drop[c * shells : (c + 1) * shells], less)
            less = density[slot, :, here] * (mask[:, away] * less)
            stage[slot, :, here] = side[d, :, here] - less
        copies.append(
            pltpu.make_async_copy(
                stage.at[slot], out.at[:, pl.ds(base, width)], marks.at[8 + slot]
            )
        )
        copies[-1].start()
    average = mean[...]
    terms = total * jnp.log(average / norm) - average * (weighted / norm)
    lane = iota((1, 128), 1)
    logs = jnp.where(lane >= 64, row[:1], 0.0)
    value = jnp.sum(terms, axis=1, keepdims=True) + jnp.sum(logs, axis=1, keepdims=True)
    loglik[...] = value / (bins * total_pix)
    for copy in copies[8:]:
        copy.wait()


def finish(
    gathered, mean, table, depth, mask, kept, given, density_kept, density_given, total_pix
):
    _, shells, width = kept.shape
    pixels, bins = 8 * width, table.shape[1]
    classes = table.shape[0] // shells
    operands = in_vmem(gathered, mean, table, depth, mask, kept, given)
    return pl.pallas_call(
        functools.partial(finish_body, classes=classes, bins=bins, total_pix=total_pix),
        in_specs=[HERE] * 7 + [AWAY] * 2,
        out_specs=[AWAY, pl.BlockSpec()],
        out_shape=[
            jax.ShapeDtypeStruct((shells, pixels), jnp.float32),
            jax.ShapeDtypeStruct((1, 1), jnp.float32),
        ],
        scratch_shapes=[
            vmem(8, shells, width),
            vmem(8, shells, width),
            pltpu.SemaphoreType.DMA((16,)),
        ],
        compiler_params=LIMIT,
        name="finish",
    )(*operands, *in_hbm(density_kept, density_given))


def gradient_body(*refs, classes, bins, mine):
    quotients, refs = refs[:4], refs[4:]
    if mine:
        density_away, rest_away, density_next, depth, weights, partner, side = refs[:7]
        out, density_there, rest_there, density, rest, marks = refs[7:]
    else:
        density, rest, depth, weights, partner, side, out = refs
    _, shells, width = out.shape
    sub = width // 2
    chip, core = position_of()
    half = core if mine else 1 - core
    loads = [()] * 4
    later = []
    if mine:

        def fetch(half, d, source, target, mark):
            base = offset_of(half, d, chip, width)
            return pltpu.make_async_copy(
                source.at[:, pl.ds(base, width)], target.at[d], marks.at[mark]
            )

        for d in range(4):
            loads[d] = (
                pltpu.make_async_copy(density_away.at[d], density.at[d], marks.at[d]),
                fetch(half, d, rest_away, rest, 4 + d),
            )
            later.append(
                pltpu.make_async_copy(density_next.at[d], density_there.at[d], marks.at[8 + d])
            )
            later.append(fetch(1 - half, d, rest_away, rest_there, 12 + d))
        for load in [load for pair in loads for load in pair] + later:
            load.start()
    row = iota((shells, WIDE), 0)
    beside_partner = (row == 0) & (core == 1) | (row == shells - 1) & (core == 0)
    outside = (row == 0) & (core == 0) | (row == shells - 1) & (core == 1)
    filler = jnp.zeros((weights.shape[1] // 3 - 2 * bins, WIDE), jnp.float32)
    for d in range(4):
        base = offset_of(half, d, chip, width)
        for load in loads[d]:
            load.wait()
        for start in range(0, sub, WIDE):
            values = quotients[d][:, start : start + WIDE]
            high, low = split(jnp.concatenate([values, filler], axis=0))
            every = jnp.dot(
                weights[...],
                jnp.concatenate([high, low, high], axis=0),
                preferred_element_type=jnp.float32,
            )
            for k in range(2):
                here = slice(start + k * sub, start + k * sub + WIDE)
                away = pl.ds(base + (start + k * sub), WIDE)
                chosen = depth[:, away]
                begin = k * classes * shells
                back = every[begin : begin + shells]
                for c in range(1, classes):
                    begin += shells
                    back = jnp.where(chosen == c, every[begin : begin + shells], back)
                near = jnp.where(beside_partner, partner[:, away], 0.0)
                near = jnp.where(outside, side[:, away], near)
                out[d, :, here] = density[d, :, here] * back + (rest[d, :, here] + RADIAL * near)
    for load in later:
        load.wait()


def gradient_kept(quotients, density, rest, next_density, common, classes, bins):
    _, shells, width = density.shape
    return pl.pallas_call(
        functools.partial(gradient_body, classes=classes, bins=bins, mine=True),
        in_specs=[HERE] * 4 + [AWAY] * 3 + [HERE] * 4,
        out_specs=[HERE] * 3,
        out_shape=[vmem(4, shells, width)] * 3,
        scratch_shapes=[
            vmem(4, shells, width),
            vmem(4, shells, width),
            pltpu.SemaphoreType.DMA((16,)),
        ],
        compiler_params=LIMIT,
        name="gradient_kept",
    )(*in_vmem(*quotients), *in_hbm(density, rest, next_density), *in_vmem(*common))


def gradient_given(quotients, density, rest, common, classes, bins):
    return pl.pallas_call(
        functools.partial(gradient_body, classes=classes, bins=bins, mine=False),
        in_specs=[HERE] * 10,
        out_specs=HERE,
        out_shape=vmem(*density.shape),
        compiler_params=LIMIT,
        name="gradient_given",
    )(*in_vmem(*quotients, density, rest, *common))


def pair_body(mine, partner, out):
    row = mine[...] + partner[...]
    out[...] = jnp.broadcast_to(row[None], out.shape)


def pair(mine, partner):
    return pl.pallas_call(
        pair_body,
        in_specs=[HERE] * 2,
        out_specs=HERE,
        out_shape=vmem(lax.axis_size("pix") * lax.axis_size("x"), 1, 128),
        compiler_params=LIMIT,
        name="pair",
    )(*in_vmem(mine, partner))


def swap(values):
    return lax.ppermute(values, "core", [(0, 1), (1, 0)])


def beside(values):
    count = lax.axis_size("x") * lax.axis_size("core")
    pairs = [(i, i + 1) for i in range(1, count - 1, 2)]
    return lax.ppermute(values, ("x", "core"), pairs + [(b, a) for a, b in pairs])


def along(values, step):
    count = lax.axis_size("x")
    return lax.ppermute(values, "x", [(i, (i + step) % count) for i in range(count)])


def across(values, start):
    pairs = [(i, i + 1) for i in range(start, lax.axis_size("pix") - 1, 2)]
    return lax.ppermute(values, "pix", pairs + [(b, a) for a, b in pairs])


def shards(field, momentum, kernels, depth_class, counts, mask, mean_counts, shell_scale):
    shells, pixels = field.shape
    classes, bins, _ = kernels.shape
    total_pix = pixels * lax.axis_size("pix")
    table = jnp.transpose(kernels, (0, 2, 1)).reshape(classes * shells, bins)

    loaded = load(
        field,
        momentum,
        depth_class.reshape(1, pixels),
        mask.reshape(1, pixels),
        table,
        classes,
        bins,
    )
    proj, density_given, place_given, field_given, momentum_given = loaded[:5]
    field_kept, momentum_kept, depth, cover, weights = loaded[5:]
    partner_far = swap(proj)
    proj, density_given, place_given = project_rest(
        field_given,
        momentum_given,
        depth,
        weights,
        density_given,
        place_given,
        False,
        classes,
        bins,
    )
    partner = swap(proj)
    second, density_kept, place_kept = project_far(
        field_kept, momentum_kept, depth, weights, partner_far, classes, bins
    )
    second = along(second, 2)
    proj, density_kept, place_kept = project_rest(
        field_kept, momentum_kept, depth, weights, density_kept, place_kept, True, classes, bins
    )
    own, first, third, near, beyond = combine(proj, partner, place_given, place_kept)
    first = along(first, 1)
    third = along(third, 3)
    near = across(near, 0)
    beyond = across(beyond, 1)
    own_counts, weights, square, mean, table, to_partner, to_side = prepare(
        counts,
        place_given,
        place_kept,
        own,
        table,
        shell_scale.reshape(1, shells),
        mean_counts.reshape(1, bins),
    )
    partner_row = swap(to_partner)
    side_row = beside(to_side)
    rest = stencil(place_given, place_kept, near, beyond, square)
    quotient, stats = ratio(own, first, second, third, own_counts, cover, rest)
    from_far = along(quotient, 2)
    from_back = along(quotient, 1)
    from_front = along(quotient, 3)
    partner_stats = swap(stats)
    stats = pair(stats, partner_stats)
    gathered = lax.all_to_all(stats, ("pix", "x"), 0, 0)
    mine = [quotient, from_front, from_far, from_back]
    theirs = [swap(q) for q in mine]

    common = (depth, weights, partner_row, side_row)
    kept, density_there, rest_there = gradient_kept(
        mine, density_kept, rest, density_given, common, classes, bins
    )
    given = gradient_given(theirs, density_there, rest_there, common, classes, bins)
    out, loglik = finish(
        gathered, mean, table, depth, cover, kept, given, density_kept, density_given, total_pix
    )
    return out, loglik.reshape(())


def solution(mesh):
    grid = mesh.devices.reshape(mesh.devices.shape[0], -1, 2)
    split_mesh = Mesh(grid, ("pix", "x", "core"))
    shell = ("x", "core")
    placed = (
        P(shell, "pix"),
        P(shell, "pix"),
        P(None, None, shell),
        P("pix"),
        P(None, "pix"),
        P("pix"),
        P(),
        P(shell),
    )
    return jax.shard_map(
        shards,
        mesh=split_mesh,
        in_specs=placed,
        out_specs=(P(shell, "pix"), P()),
        check_vma=False,
    )
```
